256 devices in a mesh: gx: 16 (over y_lo, z), gy: 4 (over x), gz: 4 (over y_hi, core).
Axes of the slice: x: 4, y: 4 (y_hi: 2, y_lo: 2; y = y_hi * 2 + y_lo), z: 8, core: 2. Of those that a mesh axis runs over, the one named last changes fastest.
Arguments:
- positions: float32 [16, 4, 4, 3, 2048], P('gx', 'gy', 'gz'), may hold values from 0 to 1
- charges: float32 [16, 4, 4, 2048], P('gx', 'gy', 'gz'), may hold values from -1.8 to 1.8
- masses: float32 [16, 4, 4, 2048], P('gx', 'gy', 'gz'), may hold values from 1 to 16
- weights: float32 [16, 4, 4, 512], P('gx', 'gy', 'gz'), may hold values from 0 to 1, as said below
- mapping: int32 [16, 4, 4, 2048], P('gx', 'gy', 'gz'), may hold values from 0 to 511, as said below
- atom_lists: int32 [16, 4, 4, 16, 27], P('gx', 'gy', 'gz'), may hold values from 0 to 431, as said below
- bead_lists: int32 [16, 4, 4, 4, 12], P('gx', 'gy', 'gz'), may hold values from 0 to 107, as said below
- leaving: int32 [16, 4, 4, 2, 128], P('gx', 'gy', 'gz'), may hold values from 0 to 511, as said below
Outputs:
- forces: float32 [16, 4, 4, 3, 2048], P('gx', 'gy', 'gz')
- arrivals: float32 [16, 4, 4, 2, 8, 128], P('gx', 'gy', 'gz')
The draws below stay inside these ranges and needn't reach their ends.
Inputs may be any that keep to these rules, and one draw needn't show every extreme that they name: `mapping`: every bead number of a cell names exactly 4 atoms of that cell. `atom_lists`: entry c of every row names a tile of neighbourhood cell c, and within one cell and one column the 16 rows name 16 different tiles. `bead_lists`: the entries of one row are distinct. `leaving`: the 256 entries of a cell are distinct. With s = (i + 0.5) / 16 for a cell at slab index i: all weights are 1 where |s - 0.5| < 0.15 and all are 0 where |s - 0.5| >= 0.35.
All inputs are finite; a program needn't handle non-finite values.
Results may differ from the reference program's by a relative error of at most 0.0003.
Values sent between devices are 32-bit elements; how exact they have to be, the bound alone decides.
A program may use at most 64 MiB of HBM per device.

```python
import math
import jax
import jax.numpy as jnp
from jax import lax

ATOMS = 2048
MOL_ATOMS = 4
LIST_BEAD = 12
BEADS = 512
ATILES = 16
BTILES = 4
LEAVERS = 128
CELLS_X = 16
CELLS_Y = 4
CELLS_Z = 4


def draw_weights(key, part):
    subkey = jax.random.fold_in(key, 11)
    shape_all = (CELLS_X, CELLS_Y, CELLS_Z, BEADS)
    middle = jax.random.uniform(subkey, shape_all, jnp.float32, 0.05, 0.95)
    slab_pos = (jnp.arange(CELLS_X, dtype=jnp.float32) + 0.5) / CELLS_X
    distance = jnp.abs(slab_pos - 0.5)[:, None, None, None]
    inner_slab = distance < 0.15
    hybrid = distance < 0.35
    return jnp.where(inner_slab, 1.0, jnp.where(hybrid, middle, 0.0)).astype(jnp.float32)


def draw_mapping(key, part):
    key_list = jax.random.split(jax.random.fold_in(key, 23), CELLS_X * CELLS_Y * CELLS_Z)
    shuffled = jax.vmap(lambda subkey: jax.random.permutation(subkey, ATOMS))(key_list)
    return (shuffled // MOL_ATOMS).astype(jnp.int32).reshape(CELLS_X, CELLS_Y, CELLS_Z, ATOMS)


def draw_atom_lists(key, part):
    key_list = jax.random.split(jax.random.fold_in(key, 37), CELLS_X * CELLS_Y * CELLS_Z * 27)
    shuffled = jax.vmap(lambda subkey: jax.random.permutation(subkey, ATILES))(key_list)
    shuffled = shuffled.reshape(CELLS_X, CELLS_Y, CELLS_Z, 27, ATILES)
    column_base = (jnp.arange(27).astype(jnp.int32) * ATILES)[:, None]
    entries = (shuffled.astype(jnp.int32) + column_base).astype(jnp.int32)
    return jnp.swapaxes(entries, 3, 4).astype(jnp.int32)


def draw_bead_lists(key, part):
    key_list = jax.random.split(jax.random.fold_in(key, 41), CELLS_X * CELLS_Y * CELLS_Z * BTILES)
    shuffled = jax.vmap(lambda subkey: jax.random.permutation(subkey, 27 * BTILES))(key_list)
    return shuffled[:, :LIST_BEAD].astype(jnp.int32).reshape(CELLS_X, CELLS_Y, CELLS_Z, BTILES, LIST_BEAD)


def draw_leaving(key, part):
    key_list = jax.random.split(jax.random.fold_in(key, 53), CELLS_X * CELLS_Y * CELLS_Z)
    shuffled = jax.vmap(lambda subkey: jax.random.permutation(subkey, BEADS))(key_list)
    return shuffled[:, :2 * LEAVERS].astype(jnp.int32).reshape(CELLS_X, CELLS_Y, CELLS_Z, 2, LEAVERS)


def block_levels(key, dims, cuts, smallest, largest):
    level = 1.0
    for dim, parts in cuts:
        steps = jax.random.uniform(jax.random.fold_in(jax.random.fold_in(key, 6), dim), (parts,), jnp.float32, smallest / len(cuts), largest / len(cuts))
        level = level * jnp.repeat(jnp.exp(steps), dims[dim] // parts).reshape((-1,) + (1,) * (len(dims) - 1 - dim))
    return level


def noise(key, extent, deviation, bound, cuts=(), kind=jnp.bfloat16):
    values = deviation * jax.random.normal(key, extent, jnp.float32)
    if cuts:
        values = values * block_levels(key, extent, cuts, -0.22, 0.18)
    return jnp.clip(values, -bound, bound).astype(kind)


def setup_inputs(seed: int = 0) -> dict:
    key_of = jax.random.split(jax.random.key(seed), 9)
    return {
        "positions": jnp.clip(1.0 * jax.random.uniform(key_of[0], (CELLS_X, CELLS_Y, CELLS_Z, 3, ATOMS), jnp.float32) ** block_levels(key_of[0], (CELLS_X, CELLS_Y, CELLS_Z, 3, ATOMS), ((0, 16), (1, 4), (2, 4)), -0.2, 0.2), 0.0, 1.0),
        "charges": noise(key_of[1], (CELLS_X, CELLS_Y, CELLS_Z, ATOMS), 0.3, 1.8, ((0, 16), (1, 4), (2, 4)), jnp.float32),
        "masses": jnp.clip(jnp.exp(math.log(16.0) - 2.7725887 * jax.random.uniform(key_of[2], (CELLS_X, CELLS_Y, CELLS_Z, ATOMS), jnp.float32) ** block_levels(key_of[2], (CELLS_X, CELLS_Y, CELLS_Z, ATOMS), ((0, 16), (1, 4), (2, 4)), -0.2, 0.2)), 1.0, 16.0),
        "weights": draw_weights(jax.random.fold_in(key_of[8], 71), 0),
        "mapping": draw_mapping(jax.random.fold_in(key_of[8], 71), 0),
        "atom_lists": draw_atom_lists(jax.random.fold_in(key_of[8], 71), 0),
        "bead_lists": draw_bead_lists(jax.random.fold_in(key_of[8], 71), 0),
        "leaving": draw_leaving(jax.random.fold_in(key_of[8], 71), 0),
    }


soft_core = 0.01
eps_coarse = 2.0
sigma_sq = 0.25

def neighbour_offsets():
    unit_steps = jnp.arange(3, dtype=jnp.float32) - 1.0
    shift_x = jnp.broadcast_to(unit_steps[:, None, None], (3, 3, 3))
    shift_y = jnp.broadcast_to(unit_steps[None, :, None], (3, 3, 3))
    shift_z = jnp.broadcast_to(unit_steps[None, None, :], (3, 3, 3))
    return jnp.stack([shift_x, shift_y, shift_z], axis=3).reshape(27, 3, 1)

def atom_tile(own_rows, listed):
    other = jnp.moveaxis(listed, 1, 0)
    displace = own_rows[:3, :, None, None] - other[:3, None, :, :]
    dist_sq = lax.optimization_barrier(jnp.sum(displace * displace, axis=0))
    inv_root = lax.rsqrt(dist_sq + soft_core)
    strength = (own_rows[3] * own_rows[4])[:, None, None] * (other[3] * other[4])[None, :, :] * (inv_root * inv_root * inv_root)
    return lax.optimization_barrier(jnp.sum(strength[None] * displace, axis=(2, 3)))

def coarse_tile(own_rows, listed):
    other = jnp.moveaxis(listed, 1, 0)
    displace = own_rows[:3, :, None, None] - other[:3, None, :, :]
    dist_sq = lax.optimization_barrier(jnp.sum(displace * displace, axis=0))
    strength = eps_coarse * jnp.exp(-dist_sq / sigma_sq) * (1.0 - own_rows[3][:, None, None] * other[3][None, :, :])
    return lax.optimization_barrier(jnp.sum(strength[None] * displace, axis=(2, 3)))

def listed_forces(near_rows, own_rows, lists, tile_fn):
    width = own_rows.shape[0]
    tile_count = own_rows.shape[1] // 128
    near_tiles = near_rows.reshape(27, width, tile_count, 128)
    own_tiles = jnp.moveaxis(own_rows.reshape(width, tile_count, 128), 1, 0)

    def one_tile(member):
        own_block, listed = member
        picked = near_tiles[listed // tile_count, :, listed % tile_count, :]
        return tile_fn(own_block, picked)
    result = lax.map(one_tile, (own_tiles, lists))
    return jnp.moveaxis(result, 0, 1).reshape(3, -1)

def reference(positions, charges, masses, weights, mapping, atom_lists, bead_lists, leaving):
    cells_x, cells_y, cells_z = (positions.shape[0], positions.shape[1], positions.shape[2])
    atom_count = positions.shape[4]
    bead_count = weights.shape[3]

    def centres_of(coords, mass, label):
        mass_sum = jax.ops.segment_sum(mass, label, num_segments=bead_count)
        centre_pos = jax.ops.segment_sum((mass[None] * coords).T, label, num_segments=bead_count).T / mass_sum
        return (centre_pos, mass_sum)
    centres, mass_sums = jax.vmap(jax.vmap(jax.vmap(centres_of)))(positions, masses, mapping)
    atom_weight = jnp.take_along_axis(weights, mapping, axis=3)
    atom_rows = jnp.concatenate([positions, charges[:, :, :, None], atom_weight[:, :, :, None]], axis=3)
    bead_rows = jnp.concatenate([centres, weights[:, :, :, None]], axis=3)
    offsets = neighbour_offsets()

    def one_cell(flat_cell):
        index_x = flat_cell // (cells_y * cells_z)
        index_y = flat_cell // cells_z % cells_y
        index_z = flat_cell % cells_z
        unit_steps = jnp.arange(3).astype(jnp.int32) - 1
        around_x = (index_x + unit_steps) % cells_x
        around_y = (index_y + unit_steps) % cells_y
        around_z = (index_z + unit_steps) % cells_z
        near_atoms = atom_rows[around_x][:, around_y][:, :, around_z].reshape(27, 5, atom_count)
        near_beads = bead_rows[around_x][:, around_y][:, :, around_z].reshape(27, 4, bead_count)
        near_atoms = near_atoms.at[:, :3].add(offsets)
        near_beads = near_beads.at[:, :3].add(offsets)
        own_atoms = atom_rows[index_x, index_y, index_z]
        own_beads = bead_rows[index_x, index_y, index_z]
        atomic_force = listed_forces(near_atoms, own_atoms, atom_lists[index_x, index_y, index_z], atom_tile)
        coarse_force = listed_forces(near_beads, own_beads, bead_lists[index_x, index_y, index_z], coarse_tile)
        label = mapping[index_x, index_y, index_z]
        fraction = masses[index_x, index_y, index_z] / mass_sums[index_x, index_y, index_z][label]
        return atomic_force + fraction[None] * coarse_force[:, label]
    total_cells = cells_x * cells_y * cells_z
    forces = lax.map(one_cell, jnp.arange(total_cells).astype(jnp.int32))
    forces = forces.reshape(cells_x, cells_y, cells_z, 3, atom_count)

    def payload_of(force, label, centre_pos, weight, mass_sum, leave):
        molecule_force = jax.ops.segment_sum(force.T, label, num_segments=bead_count).T
        record = jnp.concatenate([centre_pos, molecule_force, weight[None], mass_sum[None]], axis=0)
        return (record[:, leave[0]], record[:, leave[1]])
    upward, downward = jax.vmap(jax.vmap(jax.vmap(payload_of)))(forces, mapping, centres, weights, mass_sums, leaving)
    from_lower = jnp.roll(upward, 1, axis=0)
    from_higher = jnp.roll(downward, -1, axis=0)
    from_lower = from_lower.at[:, :, :, 0, :].add(-1.0)
    from_higher = from_higher.at[:, :, :, 0, :].add(1.0)
    arrivals = jnp.stack([from_lower, from_higher], axis=3)
    return (forces, arrivals)
```

```python
import functools

import jax
import jax.numpy as jnp
from jax import lax
from jax.experimental import pallas as pl
from jax.experimental.pallas import tpu as pltpu
from jax.sharding import PartitionSpec as P

soft_core = 0.01
inv_sigma_sq = 4.0
f32, bf16, i32 = jnp.float32, jnp.bfloat16, jnp.int32
MESH = pl.DeviceIdType.MESH
TILES = 20


def slot_of(a, b, c):
    return 9 * (a + 1) + 3 * (b + 1) + (c + 1)


OWN = slot_of(0, 0, 0)
ROUTE = {}
for _s in (-1, 1):
    ROUTE[slot_of(0, 0, _s)] = (OWN, "gz", -_s)
    for _c in (-1, 0, 1):
        ROUTE[slot_of(_s, 0, _c)] = (slot_of(0, 0, _c), "gx", -_s)
        ROUTE[slot_of(0, _s, _c)] = (slot_of(0, 0, _c), "gy", -_s)
        ROUTE[slot_of(_s, _s, _c)] = (slot_of(0, _s, _c), "gx", -_s)
        ROUTE[slot_of(-_s, _s, _c)] = (slot_of(-_s, 0, _c), "gy", -_s)

WAVES = (
    [slot_of(0, 0, c) for c in (-1, 1)]
    + [slot_of(s, 0, 0) for s in (-1, 1)]
    + [slot_of(0, s, 0) for s in (-1, 1)],
    [slot_of(s, t, 0) for s in (-1, 1) for t in (-1, 1)]
    + [slot_of(s, 0, c) for c in (-1, 1) for s in (-1, 1)]
    + [slot_of(0, s, c) for c in (-1, 1) for s in (-1, 1)],
    [slot_of(s, t, c) for c in (-1, 1) for s in (-1, 1) for t in (-1, 1)],
)


def split3(v):
    h = v.astype(bf16).astype(f32)
    r = v - h
    m = r.astype(bf16).astype(f32)
    return h, m, r - m


def dot_nt(a, b):
    return lax.dot_general(a, b, (((1,), (1,)), ((), ())), preferred_element_type=f32)


def dot_nn(a, b):
    return jnp.dot(a, b, preferred_element_type=f32)


def stack3(scr, rows, value):
    h, m, l = split3(value)
    scr[0:rows, :] = h
    scr[rows : 2 * rows, :] = m
    scr[2 * rows : 3 * rows, :] = l


def place():
    sub = lax.broadcasted_iota(i32, (10, 8, 128), 1)
    return sub & 3, sub < 4


def up_rows(x, by):
    return pltpu.roll(x, by % 8, 1)


def fourth_to_all(v, row):
    u = jnp.where(row == 3, v, 0.0)
    u = u + up_rows(u, -1)
    return u + up_rows(u, -2)


def squares_to_fourth(v):
    sq = v * v
    return up_rows(sq, 1) + up_rows(sq, 2) + up_rows(sq, 3)


def interleave(groups, low):
    even, odd = [], []
    for g, k in zip(groups[0::2], groups[1::2], strict=True):
        even.append(jnp.where(low, g, up_rows(k, 4)))
        odd.append(jnp.where(low, up_rows(g, 4), k))
    zero = jnp.zeros((10, 8, 128), f32)
    return (
        jnp.concatenate(even + [zero], axis=1),
        jnp.concatenate(odd + [zero], axis=1),
    )


def build_cell(slot, pay, bmat, rmat):
    row, low = place()
    v = pay[slot].reshape(10, 8, 128)
    offset = (slot // 9 - 1, slot // 3 % 3 - 1, slot % 3 - 1)
    for axis in range(3):
        if offset[axis]:
            v = v + jnp.where(row == axis, float(offset[axis]), 0.0)
    atoms, beads = v[:8], v[8:]
    scaled = jnp.where(row[:8] == 3, atoms, atoms * fourth_to_all(atoms, row[:8]))
    rmat[pl.ds(slot * TILES * 4, 64), :] = scaled.reshape(64, 128)
    rmat[pl.ds(slot * TILES * 4 + 64, 16), :] = beads.reshape(16, 128)
    h, m, l = split3(jnp.where(row == 3, squares_to_fourth(v), v))
    h1 = jnp.where(row == 3, 1.0, h)
    m1 = jnp.where(row == 3, 1.0, m)
    even, odd = interleave((h, h1, m, m1, l, h1), low)
    bmat[pl.ds(slot * 10, 10), 0] = even.astype(bf16)
    bmat[pl.ds(slot * 10, 10), 1] = odd.astype(bf16)


def build_own(pay, amat, wcol):
    row, low = place()
    v = pay[OWN].reshape(10, 8, 128)
    atom = lax.broadcasted_iota(i32, (10, 8, 128), 0) < 8
    near = squares_to_fourth(v) + jnp.where(atom, soft_core, 0.0)
    h, m, l = split3(jnp.where(row == 3, near, v))
    a0 = jnp.where(row == 3, 1.0, -2.0 * h)
    a1 = jnp.where(row == 3, h, -2.0 * m)
    a3 = jnp.where(row == 3, m, -2.0 * m)
    a5 = jnp.where(row == 3, l, -2.0 * l)
    even, odd = interleave((a0, a1, a0, a3, a0, a5), low)
    for t in range(TILES):
        half = (even, odd)[t % 2][t // 2]
        amat[t * 128 : t * 128 + 128, :] = half.T.astype(bf16)
    for b in range(4):
        r = 64 + 4 * b + 3
        wide = jnp.broadcast_to(pay[OWN, r : r + 1, :], (128, 128))
        wcol[b * 128 : b * 128 + 128, :] = wide.T


def distances(t, cells, lists, amat, bmat, dist):
    a = amat[pl.ds(pl.multiple_of(t * 128, 128), 128), :]
    for at in range(0, len(cells), 2):
        some = cells[at : at + 2]
        tiles = []
        for c in some:
            e = lists[0, 0, 0, t, c] + 4 * c
            tiles.append(bmat[e // 2, e % 2])
        b = tiles[0] if len(some) == 1 else jnp.concatenate(tiles, axis=1)
        dist[:, at * 128 : (at + len(some)) * 128] = dot_nn(a, b)


def add_columns(gather, first_row, rows, lane0, sums):
    lane = lax.broadcasted_iota(i32, (rows, 128), 1)
    got = gather[pl.ds(first_row, rows), :]
    for k in range(4):
        got = jnp.where(lane == lane0 + k, jnp.sum(sums[k], axis=1, keepdims=True), got)
    gather[pl.ds(first_row, rows), :] = got


def accumulate(t, cells, first, last, lists, rmat, dist, total, gather):
    rows = 32
    for g in range(128 // rows):
        at = pl.multiple_of(t * 128 + g * rows, rows)
        if first:
            acc = [jnp.zeros((rows, 128), f32) for _ in range(4)]
        else:
            acc = [total[k, pl.ds(at, rows), :] for k in range(4)]
        for n, c in enumerate(cells):
            e = 4 * (lists[0, 0, 0, t, c] + 4 * c)
            s = lax.rsqrt(dist[g * rows : (g + 1) * rows, n * 128 : n * 128 + 128])
            s = s * s * s
            for k in range(4):
                line = rmat[pl.ds(e + k, 8, stride=0), :]
                acc[k] = acc[k] + s * jnp.concatenate([line] * (rows // 8), axis=0)
        if last:
            add_columns(gather, g * rows, rows, 4 * t, acc)
        else:
            for k in range(4):
                total[k, pl.ds(at, rows), :] = acc[k]


def atomic_phase(cells, first, last, lists, amat, bmat, rmat, dist0, dist1, total, gather):
    distances(0, cells, lists, amat, bmat, dist0)

    def two_tiles(p, _):
        t = 2 * p
        distances(t + 1, cells, lists, amat, bmat, dist1)
        accumulate(t, cells, first, last, lists, rmat, dist0, total, gather)
        distances(lax.rem(t + 2, 16), cells, lists, amat, bmat, dist0)
        accumulate(t + 1, cells, first, last, lists, rmat, dist1, total, gather)
        return 0

    lax.fori_loop(0, 8, two_tiles, 0)


def coarse_phase(lists, amat, bmat, rmat, wcol, dist0, gather):
    def one(b, _):
        a = amat[pl.ds(pl.multiple_of(2048 + b * 128, 128), 128), :]
        places = []
        for n in range(12):
            e = lists[0, 0, 0, b, n]
            places.append((e // 4) * TILES + 16 + e % 4)
        for n in range(0, 12, 2):
            tiles = [bmat[q // 2, q % 2] for q in places[n : n + 2]]
            dist0[:, n * 128 : n * 128 + 256] = dot_nn(a, jnp.concatenate(tiles, axis=1))
        rows = 32
        for g in range(128 // rows):
            acc = [jnp.zeros((rows, 128), f32) for _ in range(4)]
            own = wcol[pl.ds(pl.multiple_of(b * 128 + g * rows, rows), rows), :]
            for n in range(12):
                line = [
                    jnp.concatenate([rmat[pl.ds(4 * places[n] + k, 8, stride=0), :]] * (rows // 8), axis=0)
                    for k in range(4)
                ]
                d = dist0[g * rows : (g + 1) * rows, n * 128 : n * 128 + 128]
                s = jnp.exp(-inv_sigma_sq * d) * (1.0 - own * line[3])
                for k in range(3):
                    acc[k] = acc[k] + s * line[k]
                acc[3] = acc[3] + s
            add_columns(gather, g * rows, rows, 64 + 4 * b, acc)
        return 0

    lax.fori_loop(0, 4, one, 0)


def prologue(pos, charge, mass, weight, mapping, table, pay, wide16, bead16, beads):
    label = mapping[0, 0, 0:1, :]

    def rows_of_table(k, _):
        at = pl.multiple_of(k * 32, 32)
        ids = lax.broadcasted_iota(i32, (32, 2048), 0) + at
        table[pl.ds(at, 32), :] = jnp.where(ids == label, 1.0, 0.0).astype(bf16)
        return 0

    lax.fori_loop(0, 16, rows_of_table, 0)
    wide16[12:16, :] = jnp.zeros((4, 2048), f32)
    m = mass[0, 0, 0:1, :]
    for k in range(3):
        h, mid, l = split3(m * pos[0, 0, 0, k : k + 1, :])
        wide16[k : k + 1, :] = h
        wide16[4 + k : 5 + k, :] = mid
        wide16[8 + k : 9 + k, :] = l
    h, mid, l = split3(m)
    wide16[3:4, :] = h
    wide16[7:8, :] = mid
    wide16[11:12, :] = l
    bead16[...] = dot_nt(wide16[...].astype(bf16), table[...])
    sums = bead16[0:4, :] + bead16[4:8, :] + bead16[8:12, :]
    beads[0:3, :] = sums[0:3] / sums[3:4]
    beads[6:7, :] = weight[0, 0, 0:1, :]
    beads[7:8, :] = sums[3:4]
    bead16[...] = jnp.zeros((16, 512), f32)
    h, mid, l = split3(weight[0, 0, 0:1, :])
    bead16[0:1, :] = h
    bead16[1:2, :] = mid
    bead16[2:3, :] = l
    atom_weight = jnp.sum(dot_nn(bead16[...].astype(bf16), table[...]), axis=0, keepdims=True)
    qw = charge[0, 0, 0:1, :] * atom_weight
    for t in range(16):
        cut = slice(t * 128, t * 128 + 128)
        pay[OWN, 4 * t : 4 * t + 3, :] = pos[0, 0, 0, :, cut] - 0.5
        pay[OWN, 4 * t + 3 : 4 * t + 4, :] = qw[:, cut]
    for b in range(4):
        cut = slice(b * 128, b * 128 + 128)
        pay[OWN, 64 + 4 * b : 67 + 4 * b, :] = beads[0:3, cut] - 0.5
        pay[OWN, 67 + 4 * b : 68 + 4 * b, :] = weight[0, 0, 0:1, cut]


def epilogue(mass, leaving, table, pay, gather, flat, wide16, bead16, bead32, beads, forces, parcel):
    row, _ = place()
    own = pay[OWN].reshape(10, 8, 128)
    sums = gather[...].T[0:80, :].reshape(10, 8, 128)
    force = own * fourth_to_all(sums, row) - sums
    atomic = force[:8] * fourth_to_all(own[:8], row[:8])
    flat[...] = jnp.concatenate([atomic, 2.0 * force[8:]], axis=0).reshape(80, 128)
    bead16[...] = jnp.zeros((16, 512), f32)
    for b in range(4):
        cut = slice(b * 128, b * 128 + 128)
        bead16[0:3, cut] = flat[64 + 4 * b : 67 + 4 * b, :]
    h, m, l = split3(bead16[0:3, :] / beads[7:8, :])
    bead16[0:3, :] = h
    bead16[4:7, :] = m
    bead16[8:11, :] = l
    wide16[...] = dot_nn(bead16[...].astype(bf16), table[...])
    spread = (wide16[0:3, :] + wide16[4:7, :] + wide16[8:11, :]) * mass[0, 0, 0:1, :]
    for t in range(16):
        cut = slice(t * 128, t * 128 + 128)
        forces[0, 0, 0, :, cut] = flat[4 * t : 4 * t + 3, :] + spread[:, cut]
    h, m, l = split3(forces[0, 0, 0])
    wide16[...] = jnp.zeros((16, 2048), f32)
    wide16[0:3, :] = h
    wide16[4:7, :] = m
    wide16[8:11, :] = l
    bead16[...] = dot_nt(wide16[...].astype(bf16), table[...])
    beads[3:6, :] = bead16[0:3, :] + bead16[4:7, :] + bead16[8:11, :]
    h, m, l = split3(beads[...])
    bead32[0:8, :] = h
    bead32[8:16, :] = m
    bead32[16:24, :] = l
    bead32[24:32, :] = jnp.zeros((8, 512), f32)
    rows = bead32[...].astype(bf16)
    ids = lax.broadcasted_iota(i32, (512, 128), 0)
    for way in range(2):
        pick = jnp.where(ids == leaving[0, 0, 0, way : way + 1, :], 1.0, 0.0).astype(bf16)
        got = dot_nn(rows, pick)
        parcel[way] = got[0:8] + got[8:16] + got[16:24]


def body(
    comm,
    pos, charge, mass, weight, mapping, atom_lists, bead_lists, leaving, given,
    forces, arrivals,
    pay, bmat, rmat, amat, wcol, dist0, dist1, total, gather, table, wide16, bead16, bead32, beads, flat,
    parcel, landed, send_sem, recv_sem, pass_send, pass_recv,
):
    if comm:
        me = {a: lax.axis_index(a) for a in ("gx", "gy", "gz")}
        size = {a: lax.axis_size(a) for a in ("gx", "gy", "gz")}

        def at(axis, step):
            return tuple(
                lax.rem(me[a] + (size[a] + step), size[a]) if a == axis else me[a] for a in ("gx", "gy", "gz")
            )

        barrier = pltpu.get_barrier_semaphore()
        for axis in ("gx", "gy", "gz"):
            for step in (-1, 1):
                pl.semaphore_signal(barrier, inc=1, device_id=at(axis, step), device_id_type=MESH)

        copies = {}
        for s, (source, axis, step) in ROUTE.items():
            copies[s] = pltpu.make_async_remote_copy(
                src_ref=pay.at[source],
                dst_ref=pay.at[s],
                send_sem=send_sem.at[s],
                recv_sem=recv_sem.at[s],
                device_id=at(axis, step),
                device_id_type=MESH,
            )
    prologue(pos, charge, mass, weight, mapping, table, pay, wide16, bead16, beads)
    if comm:
        pl.semaphore_wait(barrier, 6)
        for s in WAVES[0]:
            copies[s].start()
    else:
        for s in ROUTE:
            pay[s] = given[s]
    gather[...] = jnp.zeros((128, 128), f32)
    build_own(pay, amat, wcol)
    build_cell(OWN, pay, bmat, rmat)
    shared = (atom_lists, amat, bmat, rmat, dist0, dist1, total, gather)
    atomic_phase([OWN], True, False, *shared)
    for w in range(3):
        if comm:
            for s in WAVES[w]:
                copies[s].wait_recv()
            if w < 2:
                for s in WAVES[w + 1]:
                    copies[s].start()
        for s in WAVES[w]:
            build_cell(s, pay, bmat, rmat)
        atomic_phase(WAVES[w], False, w == 2, *shared)
    coarse_phase(bead_lists, amat, bmat, rmat, wcol, dist0, gather)
    epilogue(mass, leaving, table, pay, gather, flat, wide16, bead16, bead32, beads, forces, parcel)
    if comm:
        passes = []
        for way, step in ((0, 1), (1, -1)):
            passes.append(
                pltpu.make_async_remote_copy(
                    src_ref=parcel.at[way],
                    dst_ref=landed.at[way],
                    send_sem=pass_send.at[way],
                    recv_sem=pass_recv.at[way],
                    device_id=at("gx", step),
                    device_id_type=MESH,
                )
            )
            passes[-1].start()
        for s in ROUTE:
            copies[s].wait_send()
        first = lax.broadcasted_iota(i32, (8, 128), 0) == 0
        for way, move in ((0, -1.0), (1, 1.0)):
            passes[way].wait_recv()
            arrivals[0, 0, 0, way] = landed[way] + jnp.where(first, move, 0.0)
        for way in range(2):
            passes[way].wait_send()
    else:
        arrivals[0, 0, 0] = parcel[...]


def make_kernel(comm):
    vmem = pl.BlockSpec(memory_space=pltpu.VMEM)
    smem = pl.BlockSpec(memory_space=pltpu.SMEM)
    specs = [vmem] * 5 + [smem] * 2 + [vmem]
    kernel = functools.partial(body, True) if comm else functools.partial(body, False)
    if comm:

        def kernel(*refs):
            body(True, *refs[:8], None, *refs[8:])

    else:
        specs = specs + [vmem]
    return pl.pallas_call(
        kernel,
        out_shape=(
            jax.ShapeDtypeStruct((1, 1, 1, 3, 2048), f32),
            jax.ShapeDtypeStruct((1, 1, 1, 2, 8, 128), f32),
        ),
        in_specs=specs,
        out_specs=(vmem, vmem),
        scratch_shapes=[
            pltpu.VMEM((27, 80, 128), f32),
            pltpu.VMEM((270, 2, 32, 128), bf16),
            pltpu.VMEM((27 * TILES * 4, 128), f32),
            pltpu.VMEM((TILES * 128, 32), bf16),
            pltpu.VMEM((512, 128), f32),
            pltpu.VMEM((128, 12 * 128), f32),
            pltpu.VMEM((128, 12 * 128), f32),
            pltpu.VMEM((4, 2048, 128), f32),
            pltpu.VMEM((128, 128), f32),
            pltpu.VMEM((512, 2048), bf16),
            pltpu.VMEM((16, 2048), f32),
            pltpu.VMEM((16, 512), f32),
            pltpu.VMEM((32, 512), f32),
            pltpu.VMEM((8, 512), f32),
            pltpu.VMEM((80, 128), f32),
            pltpu.VMEM((2, 8, 128), f32),
            pltpu.VMEM((2, 8, 128), f32),
            pltpu.SemaphoreType.DMA((27,)),
            pltpu.SemaphoreType.DMA((27,)),
            pltpu.SemaphoreType.DMA((2,)),
            pltpu.SemaphoreType.DMA((2,)),
        ],
        compiler_params=pltpu.CompilerParams(
            collective_id=0 if comm else None, has_side_effects=comm, vmem_limit_bytes=48 << 20
        ),
        name="force_step",
    )


def solution(mesh):
    def cell(*dims):
        return P("gx", "gy", "gz", *[None] * len(dims))

    placed = (cell(0, 0), cell(0), cell(0), cell(0), cell(0), cell(0, 0), cell(0, 0), cell(0, 0))
    return jax.shard_map(
        make_kernel(True),
        mesh=mesh,
        in_specs=placed,
        out_specs=(cell(0, 0), cell(0, 0, 0)),
        check_vma=False,
    )
```

```python
import functools

import jax
import jax.numpy as jnp
from jax import lax
from jax.experimental import pallas as pl
from jax.experimental.pallas import tpu as pltpu
from jax.sharding import PartitionSpec as P

soft_core = 0.01
inv_sigma_sq = 4.0
f32, bf16, i32 = jnp.float32, jnp.bfloat16, jnp.int32
MESH = pl.DeviceIdType.MESH
TILES = 20


def slot_of(a, b, c):
    return 9 * (a + 1) + 3 * (b + 1) + (c + 1)


OWN = slot_of(0, 0, 0)
PLANE = [(a, b) for a in (-1, 0, 1) for b in (-1, 0, 1) if a or b]
POLES = [slot_of(0, 0, c) for c in (-1, 1)]
SIDES = [slot_of(a, b, 0) for a, b in PLANE]
CORNERS = [slot_of(a, b, c) for a, b in PLANE for c in (-1, 1)]
ROUTE = {slot_of(0, 0, c): (0, 0, -c) for c in (-1, 1)}
ROUTE |= {slot_of(a, b, 0): (-a, -b, 0) for a, b in PLANE}
PARTNERS = [(0, 0, -1), (0, 0, 1)] + [(a, b, 0) for a, b in PLANE]


def split3(v):
    h = v.astype(bf16).astype(f32)
    r = v - h
    m = r.astype(bf16).astype(f32)
    return h, m, r - m


def dot_nt(a, b):
    return lax.dot_general(a, b, (((1,), (1,)), ((), ())), preferred_element_type=f32)


def dot_nn(a, b):
    return jnp.dot(a, b, preferred_element_type=f32)


def stack3(scr, rows, value):
    h, m, l = split3(value)
    scr[0:rows, :] = h
    scr[rows : 2 * rows, :] = m
    scr[2 * rows : 3 * rows, :] = l


def place():
    sub = lax.broadcasted_iota(i32, (10, 8, 128), 1)
    return sub & 3, sub < 4


def up_rows(x, by):
    return pltpu.roll(x, by % 8, 1)


def fourth_to_all(v, row):
    u = jnp.where(row == 3, v, 0.0)
    u = u + up_rows(u, -1)
    return u + up_rows(u, -2)


def squares_to_fourth(v):
    sq = v * v
    return up_rows(sq, 1) + up_rows(sq, 2) + up_rows(sq, 3)


def interleave(groups, low):
    even, odd = [], []
    for g, k in zip(groups[0::2], groups[1::2], strict=True):
        even.append(jnp.where(low, g, up_rows(k, 4)))
        odd.append(jnp.where(low, up_rows(g, 4), k))
    zero = jnp.zeros((10, 8, 128), f32)
    return (
        jnp.concatenate(even + [zero], axis=1),
        jnp.concatenate(odd + [zero], axis=1),
    )


def build_cell(slot, pay, bmat, rmat):
    row, low = place()
    v = pay[slot].reshape(10, 8, 128)
    offset = (slot // 9 - 1, slot // 3 % 3 - 1, slot % 3 - 1)
    for axis in range(3):
        if offset[axis]:
            v = v + jnp.where(row == axis, float(offset[axis]), 0.0)
    atoms, beads = v[:8], v[8:]
    scaled = jnp.where(row[:8] == 3, atoms, atoms * fourth_to_all(atoms, row[:8]))
    rmat[pl.ds(slot * TILES * 4, 64), :] = scaled.reshape(64, 128)
    rmat[pl.ds(slot * TILES * 4 + 64, 16), :] = beads.reshape(16, 128)
    h, m, l = split3(jnp.where(row == 3, squares_to_fourth(v), v))
    h1 = jnp.where(row == 3, 1.0, h)
    m1 = jnp.where(row == 3, 1.0, m)
    even, odd = interleave((h, h1, m, m1, l, h1), low)
    even, odd = even.astype(bf16), odd.astype(bf16)
    for k in range(10):
        bmat[slot * TILES + 2 * k] = even[k]
        bmat[slot * TILES + 2 * k + 1] = odd[k]


def build_own(pay, amat, wcol):
    row, low = place()
    v = pay[OWN].reshape(10, 8, 128)
    atom = lax.broadcasted_iota(i32, (10, 8, 128), 0) < 8
    near = squares_to_fourth(v) + jnp.where(atom, soft_core, 0.0)
    h, m, l = split3(jnp.where(row == 3, near, v))
    a0 = jnp.where(row == 3, 1.0, -2.0 * h)
    a1 = jnp.where(row == 3, h, -2.0 * m)
    a3 = jnp.where(row == 3, m, -2.0 * m)
    a5 = jnp.where(row == 3, l, -2.0 * l)
    even, odd = interleave((a0, a1, a0, a3, a0, a5), low)
    for t in range(TILES):
        half = (even, odd)[t % 2][t // 2]
        amat[t * 128 : t * 128 + 128, :] = half.T.astype(bf16)
    for b in range(4):
        r = 64 + 4 * b + 3
        wide = jnp.broadcast_to(pay[OWN, r : r + 1, :], (128, 128))
        wcol[b * 128 : b * 128 + 128, :] = wide.T


def distance(t, some, at, lists, amat, bmat, dist):
    a = amat[pl.ds(pl.multiple_of(t * 128, 128), 128), :]
    tiles = [bmat[lists[0, 0, 0, t, c] + 4 * c] for c in some]
    b = tiles[0] if len(some) == 1 else jnp.concatenate(tiles, axis=1)
    dist[:, at * 128 : (at + len(some)) * 128] = dot_nn(a, b)


def one_tile(t, ahead, now, later, cells, first, lists, amat, bmat, rmat, total, gather):
    rows, groups = 32, 4
    pairs = range(0, len(cells), 2)
    for g in range(groups):
        if gather is not None:
            add_up((t + 15) & 15, [g], total, gather)
        at = pl.multiple_of(t * 128 + g * rows, rows)
        if first:
            acc = [jnp.zeros((rows, 128), f32) for _ in range(4)]
        else:
            acc = [total[k, pl.ds(at, rows), :] for k in range(4)]
        for p in pairs:
            turn = g * len(pairs) + p // 2
            if turn % groups == 0:
                q = 2 * (turn // groups)
                distance(ahead, cells[q : q + 2], q, lists, amat, bmat, later)
            for n in range(p, min(p + 2, len(cells))):
                e = 4 * (lists[0, 0, 0, t, cells[n]] + 4 * cells[n])
                s = lax.rsqrt(now[g * rows : (g + 1) * rows, n * 128 : n * 128 + 128])
                s = s * s * s
                for k in range(4):
                    line = rmat[pl.ds(e + k, 8, stride=0), :]
                    acc[k] = acc[k] + s * jnp.concatenate([line] * (rows // 8), axis=0)
        for k in range(4):
            total[k, pl.ds(at, rows), :] = acc[k]


def add_columns(gather, rows, lane0, sums):
    lane = lax.broadcasted_iota(i32, (rows.size, 128), 1)
    got = gather[rows, :]
    for k in range(4):
        got = jnp.where(lane == lane0 + k, jnp.sum(sums[k], axis=1, keepdims=True), got)
    gather[rows, :] = got


def add_up(t, groups, total, gather):
    for g in groups:
        at = pl.ds(pl.multiple_of(t * 128 + g * 32, 32), 32)
        add_columns(gather, pl.ds(g * 32, 32), 4 * t, [total[k, at, :] for k in range(4)])


def abs_of(x):
    return jnp.maximum(x, -x)


def when(condition, work):
    if condition is True:
        work()
    else:
        pl.when(condition)(work)


def once(p, work):
    lax.fori_loop(0, 1 + jnp.minimum(p, 0), lambda _, c: (work(), c)[1], 0)


def atomic_phase(cells, first, lists, amat, bmat, rmat, dist0, dist1, total, gather=None):
    for q in range(0, len(cells), 2):
        distance(0, cells[q : q + 2], q, lists, amat, bmat, dist0)
    shared = (cells, first, lists, amat, bmat, rmat, total, gather)

    def two_tiles(p, _):
        once(p, lambda: one_tile(2 * p, 2 * p + 1, dist0, dist1, *shared))
        once(p, lambda: one_tile(2 * p + 1, (2 * p + 2) & 15, dist1, dist0, *shared))
        return 0

    lax.fori_loop(0, 8, two_tiles, 0)
    if gather is not None:
        add_up(15, range(4), total, gather)


def coarse_phase(lists, amat, bmat, rmat, wcol, dist0, gather):
    def one(b, _):
        a = amat[pl.ds(pl.multiple_of(2048 + b * 128, 128), 128), :]
        places = []
        for n in range(12):
            e = lists[0, 0, 0, b, n]
            places.append(16 * lax.shift_right_logical(e, 2) + e + 16)
        for n in range(0, 12, 2):
            tiles = [bmat[q] for q in places[n : n + 2]]
            dist0[:, n * 128 : n * 128 + 256] = dot_nn(a, jnp.concatenate(tiles, axis=1))
        rows = 32
        for g in range(128 // rows):
            acc = [jnp.zeros((rows, 128), f32) for _ in range(4)]
            own = wcol[pl.ds(pl.multiple_of(b * 128 + g * rows, rows), rows), :]
            for n in range(12):
                line = [
                    jnp.concatenate([rmat[pl.ds(4 * places[n] + k, 8, stride=0), :]] * (rows // 8), axis=0)
                    for k in range(4)
                ]
                d = dist0[g * rows : (g + 1) * rows, n * 128 : n * 128 + 128]
                s = jnp.exp(-inv_sigma_sq * d) * (1.0 - own * line[3])
                for k in range(3):
                    acc[k] = acc[k] + s * line[k]
                acc[3] = acc[3] + s
            add_columns(gather, pl.ds(g * rows, rows), 64 + 4 * b, acc)
        return 0

    lax.fori_loop(0, 4, one, 0)


def prologue(pos, charge, mass, weight, mapping, table, pay, wide16, bead16, beads):
    label = mapping[0, 0, 0:1, :]

    def rows_of_table(k, _):
        at = pl.multiple_of(k * 32, 32)
        ids = lax.broadcasted_iota(i32, (32, 2048), 0) + at
        table[pl.ds(at, 32), :] = jnp.where(ids == label, 1.0, 0.0).astype(bf16)
        return 0

    lax.fori_loop(0, 16, rows_of_table, 0)
    wide16[12:16, :] = jnp.zeros((4, 2048), f32)
    m = mass[0, 0, 0:1, :]
    for k in range(3):
        h, mid, l = split3(m * pos[0, 0, k, 0:1, :])
        wide16[k : k + 1, :] = h
        wide16[4 + k : 5 + k, :] = mid
        wide16[8 + k : 9 + k, :] = l
    h, mid, l = split3(m)
    wide16[3:4, :] = h
    wide16[7:8, :] = mid
    wide16[11:12, :] = l
    bead16[...] = dot_nt(wide16[...].astype(bf16), table[...])
    sums = bead16[0:4, :] + bead16[4:8, :] + bead16[8:12, :]
    beads[0:3, :] = sums[0:3] / sums[3:4]
    beads[6:7, :] = weight[0, 0, 0:1, :]
    beads[7:8, :] = sums[3:4]
    bead16[...] = jnp.zeros((16, 512), f32)
    h, mid, l = split3(weight[0, 0, 0:1, :])
    bead16[0:1, :] = h
    bead16[1:2, :] = mid
    bead16[2:3, :] = l
    atom_weight = jnp.sum(dot_nn(bead16[...].astype(bf16), table[...]), axis=0, keepdims=True)
    qw = charge[0, 0, 0:1, :] * atom_weight
    for t in range(16):
        cut = slice(t * 128, t * 128 + 128)
        for k in range(3):
            pay[OWN, 4 * t + k : 4 * t + k + 1, :] = pos[0, 0, k, 0:1, cut] - 0.5
        pay[OWN, 4 * t + 3 : 4 * t + 4, :] = qw[:, cut]
    for b in range(4):
        cut = slice(b * 128, b * 128 + 128)
        pay[OWN, 64 + 4 * b : 67 + 4 * b, :] = beads[0:3, cut] - 0.5
        pay[OWN, 67 + 4 * b : 68 + 4 * b, :] = weight[0, 0, 0:1, cut]


def epilogue(leaving, table, pay, gather, flat, flat3, wide16, bead16, bead32, beads, parcel):
    row, _ = place()
    own = pay[OWN].reshape(10, 8, 128)
    summed = gather[...].T[0:80, :].reshape(10, 8, 128)
    force = own * fourth_to_all(summed, row) - summed
    atomic = force[:8] * fourth_to_all(own[:8], row[:8])
    flat[...] = jnp.concatenate([atomic, 2.0 * force[8:]], axis=0).reshape(80, 128)
    for b in range(4):
        beads[3:6, b * 128 : b * 128 + 128] = flat[64 + 4 * b : 67 + 4 * b, :]
    h, m, l = split3(beads[3:6, :] / beads[7:8, :])
    bead16[...] = jnp.zeros((16, 512), f32)
    bead16[0:3, :] = h
    bead16[4:7, :] = m
    bead16[8:11, :] = l
    coarse = bead16[...].astype(bf16)
    h, m, l = split3(atomic.reshape(64, 128))
    wide16[12:16, :] = jnp.zeros((4, 2048), f32)
    flat3[0] = h
    flat3[1] = m
    flat3[2] = l
    for t in range(16):
        cut = slice(t * 128, t * 128 + 128)
        for k in range(3):
            wide16[4 * k : 4 * k + 4, cut] = flat3[k, 4 * t : 4 * t + 4, :]
    bead16[...] = dot_nt(wide16[...].astype(bf16), table[...])
    beads[3:6, :] = beads[3:6, :] + (bead16[0:3, :] + bead16[4:7, :] + bead16[8:11, :])
    h, m, l = split3(beads[...])
    bead32[0:8, :] = h
    bead32[8:16, :] = m
    bead32[16:24, :] = l
    bead32[24:32, :] = jnp.zeros((8, 512), f32)
    rows = bead32[...].astype(bf16)
    ids = lax.broadcasted_iota(i32, (512, 128), 0)
    for way in range(2):
        pick = jnp.where(ids == leaving[0, 0, 0, way : way + 1, :], 1.0, 0.0).astype(bf16)
        got = dot_nn(rows, pick)
        parcel[way] = got[0:8] + got[8:16] + got[16:24]
    return coarse


def finish(mass, table, coarse, flat, wide16, forces):
    wide16[...] = dot_nn(coarse, table[...])
    spread = (wide16[0:3, :] + wide16[4:7, :] + wide16[8:11, :]) * mass[0, 0, 0:1, :]
    for t in range(16):
        cut = slice(t * 128, t * 128 + 128)
        got = flat[4 * t : 4 * t + 3, :] + spread[:, cut]
        for k in range(3):
            forces[0, 0, k, 0:1, cut] = got[k : k + 1]


def body(comm, *refs):
    inputs, refs = refs[:8], refs[8:]
    if not comm:
        given, refs = refs[0], refs[1:]
    (
        forces, arrivals, pos, charge, mass, weight, mapping, atom_lists, bead_lists, leaving,
        pay, bmat, rmat, amat, wcol, dist0, dist1, total, gather, table, wide16, bead16, bead32, beads, flat, flat3,
        parcel, landed, load_sem, send_sem, recv_sem, pass_send, pass_recv,
    ) = refs
    staged = (pos, charge, mass, weight, mapping, atom_lists, bead_lists, leaving)
    loads = [pltpu.make_async_copy(inputs[n], staged[n], load_sem.at[n]) for n in range(8)]
    for n in (4, 3, 2, 0, 1, 5, 6, 7):
        loads[n].start()
    if comm:
        axes = ("gx", "gy", "gz")
        me = [lax.axis_index(a) for a in axes]
        size = [lax.axis_size(a) for a in axes]

        def at(steps):
            return tuple(lax.rem(me[n] + (size[n] + steps[n]), size[n]) if steps[n] else me[n] for n in range(3))

        barrier = pltpu.get_barrier_semaphore()
        for steps in PARTNERS:
            pl.semaphore_signal(barrier, inc=1, device_id=at(steps), device_id_type=MESH)

        def send(source, target, sem, steps):
            return pltpu.make_async_remote_copy(
                src_ref=pay.at[source],
                dst_ref=pay.at[target],
                send_sem=send_sem.at[sem],
                recv_sem=recv_sem.at[sem],
                device_id=at(steps),
                device_id_type=MESH,
            )

        copies = {s: send(OWN, s, s, steps) for s, steps in ROUTE.items()}
        near = 1 - 2 * lax.rem(me[2], 2)
        other = (me[0], me[1], me[2] + near)
        far_copies, near_copies, near_arrivals = [], [], []
        for a, b in PLANE:
            side = slot_of(a, b, 0)
            far_copies.append(send(OWN - near, side - near, side - 1, (-a, -b, 0)))
            for target, group in ((side - near, near_copies), (side + near, near_arrivals)):
                group.append(
                    pltpu.make_async_remote_copy(
                        src_ref=pay.at[side],
                        dst_ref=pay.at[target],
                        send_sem=send_sem.at[side + 1],
                        recv_sem=recv_sem.at[side + 1],
                        device_id=other,
                        device_id_type=MESH,
                    )
                )
    if comm:
        away = abs_of(2 * me[0] + 1 - size[0])
        has_atomic = 10 * away < 7 * size[0]
        has_coarse = 10 * (away + 2) >= 3 * size[0]
    else:
        has_atomic = has_coarse = True
    for n in range(8):
        loads[n].wait()
    prologue(pos, charge, mass, weight, mapping, table, pay, wide16, bead16, beads)
    if comm:
        pl.semaphore_wait(barrier, len(PARTNERS))
        for s in POLES + SIDES:
            copies[s].start()
    else:
        for s in POLES + SIDES + CORNERS:
            pay[s] = given[s]
    build_own(pay, amat, wcol)
    build_cell(OWN, pay, bmat, rmat)
    shared = (atom_lists, amat, bmat, rmat, dist0, dist1, total)
    gather[...] = jnp.zeros((128, 128), f32)
    when(has_atomic, lambda: atomic_phase([OWN], True, *shared))
    if comm:
        for s in POLES:
            copies[s].wait_recv()
        for copy in far_copies:
            copy.start()
    for s in POLES:
        build_cell(s, pay, bmat, rmat)
    when(has_atomic, lambda: atomic_phase(POLES, False, *shared))
    if comm:
        for s in SIDES:
            copies[s].wait_recv()
        for copy in near_copies:
            copy.start()
    for s in SIDES:
        build_cell(s, pay, bmat, rmat)
    when(has_atomic, lambda: atomic_phase(SIDES, False, *shared))
    if comm:
        for copy in far_copies + near_arrivals:
            copy.wait_recv()
    for s in CORNERS:
        build_cell(s, pay, bmat, rmat)
    when(has_atomic, lambda: atomic_phase(CORNERS, False, *shared, gather))
    when(has_coarse, lambda: coarse_phase(bead_lists, amat, bmat, rmat, wcol, dist0, gather))
    coarse = epilogue(leaving, table, pay, gather, flat, flat3, wide16, bead16, bead32, beads, parcel)
    if comm:
        passes = []
        for way, step in ((0, 1), (1, -1)):
            passes.append(
                pltpu.make_async_remote_copy(
                    src_ref=parcel.at[way],
                    dst_ref=landed.at[way],
                    send_sem=pass_send.at[way],
                    recv_sem=pass_recv.at[way],
                    device_id=at((step, 0, 0)),
                    device_id_type=MESH,
                )
            )
            passes[-1].start()
        finish(mass, table, coarse, flat, wide16, forces)
        for copy in [*copies.values(), *far_copies, *near_copies]:
            copy.wait_send()
        first = lax.broadcasted_iota(i32, (8, 128), 0) == 0
        for way, move in ((0, -1.0), (1, 1.0)):
            passes[way].wait_recv()
            arrivals[0, 0, 0, way] = landed[way] + jnp.where(first, move, 0.0)
        for way in range(2):
            passes[way].wait_send()
    else:
        finish(mass, table, coarse, flat, wide16, forces)
        arrivals[0, 0, 0] = parcel[...]


def make_kernel(comm):
    vmem = pl.BlockSpec(memory_space=pltpu.VMEM)
    specs = [pl.BlockSpec(memory_space=pltpu.HBM)] * 8 + ([] if comm else [vmem])
    return pl.pallas_call(
        functools.partial(body, comm),
        out_shape=(
            jax.ShapeDtypeStruct((1, 1, 3, 1, 2048), f32),
            jax.ShapeDtypeStruct((1, 1, 1, 2, 8, 128), f32),
        ),
        in_specs=specs,
        out_specs=(vmem, vmem),
        scratch_shapes=[
            pltpu.VMEM((1, 1, 3, 1, 2048), f32),
            pltpu.VMEM((1, 1, 1, 2048), f32),
            pltpu.VMEM((1, 1, 1, 2048), f32),
            pltpu.VMEM((1, 1, 1, 512), f32),
            pltpu.VMEM((1, 1, 1, 2048), i32),
            pltpu.SMEM((1, 1, 1, 16, 27), i32),
            pltpu.SMEM((1, 1, 1, 4, 12), i32),
            pltpu.VMEM((1, 1, 1, 2, 128), i32),
            pltpu.VMEM((27, 80, 128), f32),
            pltpu.VMEM((27 * TILES, 32, 128), bf16),
            pltpu.VMEM((27 * TILES * 4, 128), f32),
            pltpu.VMEM((TILES * 128, 32), bf16),
            pltpu.VMEM((512, 128), f32),
            pltpu.VMEM((128, 16 * 128), f32),
            pltpu.VMEM((128, 16 * 128), f32),
            pltpu.VMEM((4, 2048, 128), f32),
            pltpu.VMEM((128, 128), f32),
            pltpu.VMEM((512, 2048), bf16),
            pltpu.VMEM((16, 2048), f32),
            pltpu.VMEM((16, 512), f32),
            pltpu.VMEM((32, 512), f32),
            pltpu.VMEM((8, 512), f32),
            pltpu.VMEM((80, 128), f32),
            pltpu.VMEM((3, 64, 128), f32),
            pltpu.VMEM((2, 8, 128), f32),
            pltpu.VMEM((2, 8, 128), f32),
            pltpu.SemaphoreType.DMA((8,)),
            pltpu.SemaphoreType.DMA((27,)),
            pltpu.SemaphoreType.DMA((27,)),
            pltpu.SemaphoreType.DMA((2,)),
            pltpu.SemaphoreType.DMA((2,)),
        ],
        compiler_params=pltpu.CompilerParams(
            collective_id=0 if comm else None, has_side_effects=comm, vmem_limit_bytes=48 << 20
        ),
        name="force_step",
    )


def solution(mesh):
    def cell(*dims):
        return P("gx", "gy", "gz", *[None] * len(dims))

    placed = (cell(0, 0), cell(0), cell(0), cell(0), cell(0), cell(0, 0), cell(0, 0), cell(0, 0))
    def step(positions, *rest):
        operands = [pltpu.with_memory_space_constraint(x, pltpu.HBM) for x in (jnp.swapaxes(positions, 2, 3), *rest)]
        forces, arrivals = make_kernel(True)(*operands)
        return jnp.swapaxes(forces, 2, 3), arrivals

    return jax.shard_map(
        step,
        mesh=mesh,
        in_specs=placed,
        out_specs=(cell(0, 0), cell(0, 0, 0)),
        check_vma=False,
    )
```

```python
import functools

import jax
import jax.numpy as jnp
from jax import lax
from jax.experimental import pallas as pl
from jax.experimental.pallas import tpu as pltpu
from jax.sharding import PartitionSpec as P

soft_core = 0.01
inv_sigma_sq = 4.0
log2_e = 1.4426950408889634
f32, bf16, i32 = jnp.float32, jnp.bfloat16, jnp.int32
MESH = pl.DeviceIdType.MESH
TILES = 20


def slot_of(a, b, c):
    return 9 * (a + 1) + 3 * (b + 1) + (c + 1)


OWN = slot_of(0, 0, 0)
PLANE = [(a, b) for a in (-1, 0, 1) for b in (-1, 0, 1) if a or b]
POLES = [slot_of(0, 0, c) for c in (-1, 1)]
SIDES = [slot_of(a, b, 0) for a, b in PLANE]
CORNERS = [slot_of(a, b, c) for a, b in PLANE for c in (-1, 1)]
ROUTE = {slot_of(0, 0, c): (0, 0, -c) for c in (-1, 1)}
ROUTE |= {slot_of(a, b, 0): (-a, -b, 0) for a, b in PLANE}
PARTNERS = [(0, 0, -1), (0, 0, 1)] + [(a, b, 0) for a, b in PLANE]


def split3(v):
    h = v.astype(bf16).astype(f32)
    r = v - h
    m = r.astype(bf16).astype(f32)
    return h, m, r - m


def dot_nt(a, b):
    return lax.dot_general(a, b, (((1,), (1,)), ((), ())), preferred_element_type=f32)


def dot_nn(a, b):
    return jnp.dot(a, b, preferred_element_type=f32)


def stack3(scr, rows, value):
    h, m, l = split3(value)
    scr[0:rows, :] = h
    scr[rows : 2 * rows, :] = m
    scr[2 * rows : 3 * rows, :] = l


def place():
    sub = lax.broadcasted_iota(i32, (10, 8, 128), 1)
    return sub & 3, sub < 4


def up_rows(x, by):
    return pltpu.roll(x, by % 8, 1)


def fourth_to_all(v, row):
    u = jnp.where(row == 3, v, 0.0)
    u = u + up_rows(u, -1)
    return u + up_rows(u, -2)


def squares_to_fourth(v):
    sq = v * v
    return up_rows(sq, 1) + up_rows(sq, 2) + up_rows(sq, 3)


def interleave(groups, low):
    even, odd = [], []
    for g, k in zip(groups[0::2], groups[1::2], strict=True):
        even.append(jnp.where(low, g, up_rows(k, 4)))
        odd.append(jnp.where(low, up_rows(g, 4), k))
    zero = jnp.zeros((10, 8, 128), f32)
    return (
        jnp.concatenate(even + [zero], axis=1),
        jnp.concatenate(odd + [zero], axis=1),
    )


def build_cell(slot, pay, bmat, rmat):
    row, low = place()
    v = pay[slot].reshape(10, 8, 128)
    offset = (slot // 9 - 1, slot // 3 % 3 - 1, slot % 3 - 1)
    for axis in range(3):
        if offset[axis]:
            v = v + jnp.where(row == axis, float(offset[axis]), 0.0)
    atoms, beads = v[:8], v[8:]
    scaled = jnp.where(row[:8] == 3, atoms, atoms * fourth_to_all(atoms, row[:8]))
    rmat[pl.ds(slot * TILES * 4, 64), :] = scaled.reshape(64, 128)
    rmat[pl.ds(slot * TILES * 4 + 64, 16), :] = beads.reshape(16, 128)
    h, m, l = split3(jnp.where(row == 3, squares_to_fourth(v), v))
    h1 = jnp.where(row == 3, 1.0, h)
    m1 = jnp.where(row == 3, 1.0, m)
    even, odd = interleave((h, h1, m, m1, l, h1), low)
    even, odd = even.astype(bf16), odd.astype(bf16)
    for k in range(10):
        bmat[slot * TILES + 2 * k] = even[k]
        bmat[slot * TILES + 2 * k + 1] = odd[k]


def build_own(pay, amat, wcol):
    row, low = place()
    v = pay[OWN].reshape(10, 8, 128)
    atom = lax.broadcasted_iota(i32, (10, 8, 128), 0) < 8
    near = squares_to_fourth(v) + jnp.where(atom, soft_core, 0.0)
    h, m, l = split3(jnp.where(row == 3, near, v))
    a0 = jnp.where(row == 3, 1.0, -2.0 * h)
    a1 = jnp.where(row == 3, h, -2.0 * m)
    a3 = jnp.where(row == 3, m, -2.0 * m)
    a5 = jnp.where(row == 3, l, -2.0 * l)
    even, odd = interleave((a0, a1, a0, a3, a0, a5), low)
    for t in range(TILES):
        half = (even, odd)[t % 2][t // 2]
        amat[t * 128 : t * 128 + 128, :] = half.T.astype(bf16)
    for b in range(4):
        r = 64 + 4 * b + 3
        wide = jnp.broadcast_to(pay[OWN, r : r + 1, :], (128, 128))
        wcol[b * 128 : b * 128 + 128, :] = wide.T


def distance(t, some, at, lists, amat, bmat, dist):
    a = amat[pl.ds(pl.multiple_of(t * 128, 128), 128), :]
    tiles = [bmat[lists[0, 0, 0, t, c] + 4 * c] for c in some]
    b = tiles[0] if len(some) == 1 else jnp.concatenate(tiles, axis=1)
    dist[:, at * 128 : (at + len(some)) * 128] = dot_nn(a, b)


def one_tile(t, ahead, now, later, cells, first, lists, amat, bmat, rmat, total, gather, before=None, done=None):
    rows, groups = 32, 4
    pairs = range(0, len(cells), 2)
    for g in range(groups):
        if gather is not None:
            add_up((t + 15) & 15, [g], before, gather)
        at = pl.multiple_of(t * 128 + g * rows, rows)
        if first:
            acc = [jnp.zeros((rows, 128), f32) for _ in range(4)]
        else:
            acc = [total[k, pl.ds(at, rows), :] for k in range(4)]
        for p in pairs:
            turn = g * len(pairs) + p // 2
            if turn % groups == 0:
                q = 2 * (turn // groups)
                distance(ahead, cells[q : q + 2], q, lists, amat, bmat, later)
            for n in range(p, min(p + 2, len(cells))):
                e = 4 * (lists[0, 0, 0, t, cells[n]] + 4 * cells[n])
                s = lax.rsqrt(now[g * rows : (g + 1) * rows, n * 128 : n * 128 + 128])
                s = s * s * s
                for k in range(4):
                    line = rmat[pl.ds(e + k, 8, stride=0), :]
                    acc[k] = acc[k] + s * jnp.concatenate([line] * (rows // 8), axis=0)
        for k in range(4):
            if done is None:
                total[k, pl.ds(at, rows), :] = acc[k]
            else:
                done[k, g * rows : (g + 1) * rows, :] = acc[k]


def add_columns(gather, rows, lane0, sums):
    lane = lax.broadcasted_iota(i32, (rows.size, 128), 1)
    got = gather[rows, :]
    for k in range(4):
        got = jnp.where(lane == lane0 + k, jnp.sum(sums[k], axis=1, keepdims=True), got)
    gather[rows, :] = got


def add_up(t, groups, done, gather):
    for g in groups:
        at = pl.ds(g * 32, 32)
        add_columns(gather, at, 4 * t, [done[k, at, :] for k in range(4)])


def abs_of(x):
    return jnp.maximum(x, -x)


def when(condition, work):
    if condition is True:
        work()
    else:
        pl.when(condition)(work)


def once(p, work):
    lax.fori_loop(0, 1 + jnp.minimum(p, 0), lambda _, c: (work(), c)[1], 0)


def atomic_phase(cells, first, lists, amat, bmat, rmat, dist0, dist1, total, gather=None, done=(None, None)):
    for q in range(0, len(cells), 2):
        distance(0, cells[q : q + 2], q, lists, amat, bmat, dist0)
    shared = (cells, first, lists, amat, bmat, rmat, total, gather)

    def two_tiles(p, _):
        once(p, lambda: one_tile(2 * p, 2 * p + 1, dist0, dist1, *shared, done[1], done[0]))
        once(p, lambda: one_tile(2 * p + 1, (2 * p + 2) & 15, dist1, dist0, *shared, done[0], done[1]))
        return 0

    lax.fori_loop(0, 8, two_tiles, 0)
    if gather is not None:
        add_up(15, range(4), done[1], gather)


def bead_places(lists, b):
    return [16 * lax.shift_right_logical(lists[0, 0, 0, b, n], 2) + lists[0, 0, 0, b, n] + 16 for n in range(12)]


def bead_distances(b, n, lists, amat, bmat, dist):
    a = amat[2048 + b * 128 : 2176 + b * 128, :]
    tiles = [bmat[q] for q in bead_places(lists, b)[n : n + 2]]
    dist[:, n * 128 : n * 128 + 256] = dot_nn(a, jnp.concatenate(tiles, axis=1))


def bead_tile(b, now, later, lists, amat, bmat, rmat, wcol, gather):
    rows = 32
    places = bead_places(lists, b)
    for g in range(128 // rows):
        acc = [jnp.zeros((rows, 128), f32) for _ in range(4)]
        own = wcol[b * 128 + g * rows : b * 128 + (g + 1) * rows, :]
        for n in range(12):
            if b < 3 and n % 2 == 0 and (6 * g + n // 2) % 4 == 0:
                bead_distances(b + 1, 2 * ((6 * g + n // 2) // 4), lists, amat, bmat, later)
            line = [
                jnp.concatenate([rmat[pl.ds(4 * places[n] + k, 8, stride=0), :]] * (rows // 8), axis=0) for k in range(4)
            ]
            d = now[g * rows : (g + 1) * rows, n * 128 : n * 128 + 128]
            s = jnp.exp2((-inv_sigma_sq * log2_e) * d) * (1.0 - own * line[3])
            for k in range(3):
                acc[k] = acc[k] + s * line[k]
            acc[3] = acc[3] + s
        add_columns(gather, pl.ds(g * rows, rows), 64 + 4 * b, acc)


def coarse_phase(lists, amat, bmat, rmat, wcol, dist0, dist1, gather):
    for n in range(0, 12, 2):
        bead_distances(0, n, lists, amat, bmat, dist0)
    for b in range(4):
        bead_tile(b, (dist0, dist1)[b % 2], (dist1, dist0)[b % 2], lists, amat, bmat, rmat, wcol, gather)


def prologue(pos, charge, mass, weight, mapping, table, pay, wide16, bead16, light16, beads):
    label = mapping[0, 0, 0:1, :]

    label16 = label.astype(jnp.int16)

    def rows_of_table(k, _):
        at = pl.multiple_of(k * 32, 32)
        ids = (lax.broadcasted_iota(i32, (32, 2048), 0) + at).astype(jnp.int16)
        same = ids == jnp.broadcast_to(label16, (32, 2048))
        table[pl.ds(at, 32), :] = jnp.where(same, jnp.ones((), bf16), jnp.zeros((), bf16))
        return 0

    lax.fori_loop(0, 16, rows_of_table, 0)
    wide16[12:16, :] = jnp.zeros((4, 2048), f32)
    m = mass[0, 0, 0:1, :]
    for k in range(3):
        h, mid, l = split3(m * pos[0, 0, k, 0:1, :])
        wide16[k : k + 1, :] = h
        wide16[4 + k : 5 + k, :] = mid
        wide16[8 + k : 9 + k, :] = l
    h, mid, l = split3(m)
    wide16[3:4, :] = h
    wide16[7:8, :] = mid
    wide16[11:12, :] = l
    bead16[...] = dot_nt(wide16[...].astype(bf16), table[...])
    sums = bead16[0:4, :] + bead16[4:8, :] + bead16[8:12, :]
    beads[0:3, :] = sums[0:3] / sums[3:4]
    beads[6:7, :] = weight[0, 0, 0:1, :]
    beads[7:8, :] = sums[3:4]
    light16[...] = jnp.zeros((16, 512), f32)
    h, mid, l = split3(weight[0, 0, 0:1, :])
    light16[0:1, :] = h
    light16[1:2, :] = mid
    light16[2:3, :] = l
    atom_weight = jnp.sum(dot_nn(light16[...].astype(bf16), table[...]), axis=0, keepdims=True)
    qw = charge[0, 0, 0:1, :] * atom_weight
    for t in range(16):
        cut = slice(t * 128, t * 128 + 128)
        for k in range(3):
            pay[OWN, 4 * t + k : 4 * t + k + 1, :] = pos[0, 0, k, 0:1, cut] - 0.5
        pay[OWN, 4 * t + 3 : 4 * t + 4, :] = qw[:, cut]
    for b in range(4):
        cut = slice(b * 128, b * 128 + 128)
        pay[OWN, 64 + 4 * b : 67 + 4 * b, :] = beads[0:3, cut] - 0.5
        pay[OWN, 67 + 4 * b : 68 + 4 * b, :] = weight[0, 0, 0:1, cut]


def build_leavers(leaving, mapping, picks, leavers):
    ids = lax.broadcasted_iota(i32, (512, 128), 0)
    for way in range(2):
        row = leaving[0, 0, 0, way : way + 1, :]
        picks[:, way * 128 : way * 128 + 128] = jnp.where(ids == row, 1.0, 0.0).astype(bf16)
        column = jnp.broadcast_to(row.astype(f32), (128, 128)).T.astype(i32)
        for t in range(16):
            cut = slice(t * 128, t * 128 + 128)
            leavers[way * 128 : way * 128 + 128, cut] = jnp.where(column == mapping[0, 0, 0:1, cut], 1.0, 0.0).astype(bf16)


def epilogue(pay, gather, picks, leavers, flat, flat3, wide16, bead16, bead32, beads, parcel):
    row, _ = place()
    own = pay[OWN].reshape(10, 8, 128)
    summed = gather[...].T[0:80, :].reshape(10, 8, 128)
    force = own * fourth_to_all(summed, row) - summed
    atomic = force[:8] * fourth_to_all(own[:8], row[:8])
    flat[...] = jnp.concatenate([atomic, 2.0 * force[8:]], axis=0).reshape(80, 128)
    h, m, l = split3(atomic.reshape(64, 128))
    flat3[0] = h
    flat3[1] = m
    flat3[2] = l
    wide16[12:16, :] = jnp.zeros((4, 2048), f32)
    for t in range(16):
        cut = slice(t * 128, t * 128 + 128)
        for k in range(3):
            wide16[4 * k : 4 * k + 4, cut] = flat3[k, 4 * t : 4 * t + 4, :]
    summed = dot_nt(wide16[...].astype(bf16), leavers[...])
    for b in range(4):
        beads[3:6, b * 128 : b * 128 + 128] = flat[64 + 4 * b : 67 + 4 * b, :]
    h, m, l = split3(beads[...])
    bead32[0:8, :] = h
    bead32[8:16, :] = m
    bead32[16:24, :] = l
    bead32[24:32, :] = jnp.zeros((8, 512), f32)
    got = dot_nn(bead32[...].astype(bf16), picks[...])
    got = got[0:8] + got[8:16] + got[16:24]
    bead16[:, 0:256] = summed
    for way in range(2):
        cut = slice(way * 128, way * 128 + 128)
        parcel[way] = got[:, cut]
        parcel[way, 3:6, :] = parcel[way, 3:6, :] + (bead16[0:3, cut] + bead16[4:7, cut] + bead16[8:11, cut])
    h, m, l = split3(beads[3:6, :] / beads[7:8, :])
    bead16[...] = jnp.zeros((16, 512), f32)
    bead16[0:3, :] = h
    bead16[4:7, :] = m
    bead16[8:11, :] = l
    return bead16[...].astype(bf16)


def finish(mass, table, coarse, flat, wide16, forces):
    wide16[...] = dot_nn(coarse, table[...])
    spread = (wide16[0:3, :] + wide16[4:7, :] + wide16[8:11, :]) * mass[0, 0, 0:1, :]
    for t in range(16):
        cut = slice(t * 128, t * 128 + 128)
        got = flat[4 * t : 4 * t + 3, :] + spread[:, cut]
        for k in range(3):
            forces[0, 0, k, 0:1, cut] = got[k : k + 1]


def body(comm, *refs):
    inputs, refs = refs[:8], refs[8:]
    if not comm:
        given, refs = refs[0], refs[1:]
    (
        forces, arrivals, pos, charge, mass, weight, mapping, atom_lists, bead_lists, leaving,
        pay, bmat, rmat, amat, wcol, dist0, dist1, done0, done1, total, gather, table, wide16, bead16, light16, bead32, beads, picks, leavers, flat, flat3,
        parcel, landed, load_sem, send_sem, recv_sem, pass_send, pass_recv,
    ) = refs
    staged = (pos, charge, mass, weight, mapping, atom_lists, bead_lists, leaving)
    loads = [pltpu.make_async_copy(inputs[n], staged[n], load_sem.at[n]) for n in range(8)]
    for n in (4, 3, 2, 0, 1, 5, 6, 7):
        loads[n].start()
    if comm:
        axes = ("gx", "gy", "gz")
        me = [lax.axis_index(a) for a in axes]
        size = [lax.axis_size(a) for a in axes]

        def at(steps):
            return tuple(lax.rem(me[n] + (size[n] + steps[n]), size[n]) if steps[n] else me[n] for n in range(3))

        barrier = pltpu.get_barrier_semaphore()
        for steps in PARTNERS:
            pl.semaphore_signal(barrier, inc=1, device_id=at(steps), device_id_type=MESH)

        def send(source, target, sem, steps):
            return pltpu.make_async_remote_copy(
                src_ref=pay.at[source],
                dst_ref=pay.at[target],
                send_sem=send_sem.at[sem],
                recv_sem=recv_sem.at[sem],
                device_id=at(steps),
                device_id_type=MESH,
            )

        copies = {s: send(OWN, s, s, steps) for s, steps in ROUTE.items()}
        near = 1 - 2 * lax.rem(me[2], 2)
        other = (me[0], me[1], me[2] + near)
        far_copies, near_copies, near_arrivals = [], [], []
        for a, b in PLANE:
            side = slot_of(a, b, 0)
            far_copies.append(send(OWN - near, side - near, side - 1, (-a, -b, 0)))
            for target, group in ((side - near, near_copies), (side + near, near_arrivals)):
                group.append(
                    pltpu.make_async_remote_copy(
                        src_ref=pay.at[side],
                        dst_ref=pay.at[target],
                        send_sem=send_sem.at[side + 1],
                        recv_sem=recv_sem.at[side + 1],
                        device_id=other,
                        device_id_type=MESH,
                    )
                )
    if comm:
        away = abs_of(2 * me[0] + 1 - size[0])
        has_atomic = 10 * away < 7 * size[0]
        has_coarse = 10 * (away + 2) >= 3 * size[0]
    else:
        has_atomic = has_coarse = True
    for n in range(8):
        loads[n].wait()
    prologue(pos, charge, mass, weight, mapping, table, pay, wide16, bead16, light16, beads)
    if comm:
        pl.semaphore_wait(barrier, len(PARTNERS))
        for s in POLES + SIDES:
            copies[s].start()
    else:
        for s in POLES + SIDES + CORNERS:
            pay[s] = given[s]
    build_own(pay, amat, wcol)
    build_leavers(leaving, mapping, picks, leavers)
    build_cell(OWN, pay, bmat, rmat)
    shared = (atom_lists, amat, bmat, rmat, dist0, dist1, total)
    gather[...] = jnp.zeros((128, 128), f32)
    when(has_atomic, lambda: atomic_phase([OWN], True, *shared))
    if comm:
        for s in POLES:
            copies[s].wait_recv()
        for copy in far_copies:
            copy.start()
    for s in POLES:
        build_cell(s, pay, bmat, rmat)
    when(has_atomic, lambda: atomic_phase(POLES, False, *shared))
    if comm:
        for s in SIDES:
            copies[s].wait_recv()
        for copy in near_copies:
            copy.start()
    for s in SIDES:
        build_cell(s, pay, bmat, rmat)
    when(has_atomic, lambda: atomic_phase(SIDES, False, *shared))
    if comm:
        for copy in far_copies + near_arrivals:
            copy.wait_recv()
    for s in CORNERS:
        build_cell(s, pay, bmat, rmat)
    when(has_atomic, lambda: atomic_phase(CORNERS, False, *shared, gather, (done0, done1)))
    when(has_coarse, lambda: coarse_phase(bead_lists, amat, bmat, rmat, wcol, dist0, dist1, gather))
    coarse = epilogue(pay, gather, picks, leavers, flat, flat3, wide16, bead16, bead32, beads, parcel)
    if comm:
        passes = []
        for way, step in ((0, 1), (1, -1)):
            passes.append(
                pltpu.make_async_remote_copy(
                    src_ref=parcel.at[way],
                    dst_ref=landed.at[way],
                    send_sem=pass_send.at[way],
                    recv_sem=pass_recv.at[way],
                    device_id=at((step, 0, 0)),
                    device_id_type=MESH,
                )
            )
            passes[-1].start()
        finish(mass, table, coarse, flat, wide16, forces)
        for copy in [*copies.values(), *far_copies, *near_copies]:
            copy.wait_send()
        first = lax.broadcasted_iota(i32, (8, 128), 0) == 0
        for way, move in ((0, -1.0), (1, 1.0)):
            passes[way].wait_recv()
            arrivals[0, 0, 0, way] = landed[way] + jnp.where(first, move, 0.0)
        for way in range(2):
            passes[way].wait_send()
    else:
        finish(mass, table, coarse, flat, wide16, forces)
        arrivals[0, 0, 0] = parcel[...]


def make_kernel(comm):
    vmem = pl.BlockSpec(memory_space=pltpu.VMEM)
    specs = [pl.BlockSpec(memory_space=pltpu.HBM)] * 8 + ([] if comm else [vmem])
    return pl.pallas_call(
        functools.partial(body, comm),
        out_shape=(
            jax.ShapeDtypeStruct((1, 1, 3, 1, 2048), f32),
            jax.ShapeDtypeStruct((1, 1, 1, 2, 8, 128), f32),
        ),
        in_specs=specs,
        out_specs=(vmem, vmem),
        scratch_shapes=[
            pltpu.VMEM((1, 1, 3, 1, 2048), f32),
            pltpu.VMEM((1, 1, 1, 2048), f32),
            pltpu.VMEM((1, 1, 1, 2048), f32),
            pltpu.VMEM((1, 1, 1, 512), f32),
            pltpu.VMEM((1, 1, 1, 2048), i32),
            pltpu.SMEM((1, 1, 1, 16, 27), i32),
            pltpu.SMEM((1, 1, 1, 4, 12), i32),
            pltpu.VMEM((1, 1, 1, 2, 128), i32),
            pltpu.VMEM((27, 80, 128), f32),
            pltpu.VMEM((27 * TILES, 32, 128), bf16),
            pltpu.VMEM((27 * TILES * 4, 128), f32),
            pltpu.VMEM((TILES * 128, 32), bf16),
            pltpu.VMEM((512, 128), f32),
            pltpu.VMEM((128, 16 * 128), f32),
            pltpu.VMEM((128, 16 * 128), f32),
            pltpu.VMEM((4, 128, 128), f32),
            pltpu.VMEM((4, 128, 128), f32),
            pltpu.VMEM((4, 2048, 128), f32),
            pltpu.VMEM((128, 128), f32),
            pltpu.VMEM((512, 2048), bf16),
            pltpu.VMEM((16, 2048), f32),
            pltpu.VMEM((16, 512), f32),
            pltpu.VMEM((16, 512), f32),
            pltpu.VMEM((32, 512), f32),
            pltpu.VMEM((8, 512), f32),
            pltpu.VMEM((512, 256), bf16),
            pltpu.VMEM((256, 2048), bf16),
            pltpu.VMEM((80, 128), f32),
            pltpu.VMEM((3, 64, 128), f32),
            pltpu.VMEM((2, 8, 128), f32),
            pltpu.VMEM((2, 8, 128), f32),
            pltpu.SemaphoreType.DMA((8,)),
            pltpu.SemaphoreType.DMA((27,)),
            pltpu.SemaphoreType.DMA((27,)),
            pltpu.SemaphoreType.DMA((2,)),
            pltpu.SemaphoreType.DMA((2,)),
        ],
        compiler_params=pltpu.CompilerParams(
            collective_id=0 if comm else None, has_side_effects=comm, vmem_limit_bytes=48 << 20
        ),
        name="force_step",
    )


def put_out(forces, arrivals, forces_out, arrivals_out, sem):
    copies = [
        pltpu.make_async_copy(forces, forces_out, sem.at[0]),
        pltpu.make_async_copy(arrivals, arrivals_out, sem.at[1]),
    ]
    for copy in copies:
        copy.start()
    for copy in copies:
        copy.wait()


def settle(forces, arrivals):
    vmem = pl.BlockSpec(memory_space=pltpu.VMEM)
    hbm = pl.BlockSpec(memory_space=pltpu.HBM)
    return pl.pallas_call(
        put_out,
        out_shape=(
            jax.ShapeDtypeStruct(forces.shape, f32),
            jax.ShapeDtypeStruct(arrivals.shape, f32),
        ),
        in_specs=[vmem, vmem],
        out_specs=(hbm, hbm),
        scratch_shapes=[pltpu.SemaphoreType.DMA((2,))],
        compiler_params=pltpu.CompilerParams(vmem_limit_bytes=8 << 20),
        name="settle",
    )(forces, arrivals)


def solution(mesh):
    def cell(*dims):
        return P("gx", "gy", "gz", *[None] * len(dims))

    placed = (cell(0, 0), cell(0), cell(0), cell(0), cell(0), cell(0, 0), cell(0, 0), cell(0, 0))
    def step(positions, *rest):
        operands = [pltpu.with_memory_space_constraint(x, pltpu.HBM) for x in (jnp.swapaxes(positions, 2, 3), *rest)]
        forces, arrivals = settle(*make_kernel(True)(*operands))
        return jnp.swapaxes(forces, 2, 3), arrivals

    return jax.shard_map(
        step,
        mesh=mesh,
        in_specs=placed,
        out_specs=(cell(0, 0), cell(0, 0, 0)),
        check_vma=False,
    )
```

```python
import functools

import jax
import jax.numpy as jnp
from jax import lax
from jax.experimental import pallas as pl
from jax.experimental.pallas import tpu as pltpu
from jax.sharding import PartitionSpec as P

soft_core = 0.01
inv_sigma_sq = 4.0
log2_e = 1.4426950408889634
f32, bf16, i32 = jnp.float32, jnp.bfloat16, jnp.int32
MESH = pl.DeviceIdType.MESH
TILES = 20


def slot_of(a, b, c):
    return 9 * (a + 1) + 3 * (b + 1) + (c + 1)


OWN = slot_of(0, 0, 0)
PLANE = [(a, b) for a in (-1, 0, 1) for b in (-1, 0, 1) if a or b]
POLES = [slot_of(0, 0, c) for c in (-1, 1)]
SIDES = [slot_of(a, b, 0) for a, b in PLANE]
CORNERS = [slot_of(a, b, c) for a, b in PLANE for c in (-1, 1)]
ROUTE = {slot_of(0, 0, c): (0, 0, -c) for c in (-1, 1)}
ROUTE |= {slot_of(a, b, 0): (-a, -b, 0) for a, b in PLANE}
PARTNERS = [(0, 0, -1), (0, 0, 1)] + [(a, b, 0) for a, b in PLANE]


def split3(v):
    h = v.astype(bf16).astype(f32)
    r = v - h
    m = r.astype(bf16).astype(f32)
    return h, m, r - m


def dot_nt(a, b):
    return lax.dot_general(a, b, (((1,), (1,)), ((), ())), preferred_element_type=f32)


def dot_nn(a, b):
    return jnp.dot(a, b, preferred_element_type=f32)


def stack3(scr, rows, value):
    h, m, l = split3(value)
    scr[0:rows, :] = h
    scr[rows : 2 * rows, :] = m
    scr[2 * rows : 3 * rows, :] = l


def place():
    sub = lax.broadcasted_iota(i32, (10, 8, 128), 1)
    return sub & 3, sub < 4


def up_rows(x, by):
    return pltpu.roll(x, by % 8, 1)


def fourth_to_all(v, row):
    u = jnp.where(row == 3, v, 0.0)
    u = u + up_rows(u, -1)
    return u + up_rows(u, -2)


def squares_to_fourth(v):
    sq = v * v
    return up_rows(sq, 1) + up_rows(sq, 2) + up_rows(sq, 3)


def interleave(groups, low):
    even, odd = [], []
    for g, k in zip(groups[0::2], groups[1::2], strict=True):
        even.append(jnp.where(low, g, up_rows(k, 4)))
        odd.append(jnp.where(low, up_rows(g, 4), k))
    zero = jnp.zeros((10, 8, 128), f32)
    return (
        jnp.concatenate(even + [zero], axis=1),
        jnp.concatenate(odd + [zero], axis=1),
    )


def build_cell(slot, pay, bmat, rmat):
    row, low = place()
    v = pay[slot].reshape(10, 8, 128)
    offset = (slot // 9 - 1, slot // 3 % 3 - 1, slot % 3 - 1)
    for axis in range(3):
        if offset[axis]:
            v = v + jnp.where(row == axis, float(offset[axis]), 0.0)
    atoms, beads = v[:8], v[8:]
    scaled = jnp.where(row[:8] == 3, atoms, atoms * fourth_to_all(atoms, row[:8]))
    rmat[pl.ds(slot * TILES * 4, 64), :] = scaled.reshape(64, 128)
    rmat[pl.ds(slot * TILES * 4 + 64, 16), :] = beads.reshape(16, 128)
    h, m, l = split3(jnp.where(row == 3, squares_to_fourth(v), v))
    h1 = jnp.where(row == 3, 1.0, h)
    m1 = jnp.where(row == 3, 1.0, m)
    even, odd = interleave((h, h1, m, m1, l, h1), low)
    even, odd = even.astype(bf16), odd.astype(bf16)
    for k in range(10):
        bmat[slot * TILES + 2 * k] = even[k]
        bmat[slot * TILES + 2 * k + 1] = odd[k]


def build_own(pay, amat, wcol):
    row, low = place()
    v = pay[OWN].reshape(10, 8, 128)
    atom = lax.broadcasted_iota(i32, (10, 8, 128), 0) < 8
    near = squares_to_fourth(v) + jnp.where(atom, soft_core, 0.0)
    h, m, l = split3(jnp.where(row == 3, near, v))
    a0 = jnp.where(row == 3, 1.0, -2.0 * h)
    a1 = jnp.where(row == 3, h, -2.0 * m)
    a3 = jnp.where(row == 3, m, -2.0 * m)
    a5 = jnp.where(row == 3, l, -2.0 * l)
    even, odd = interleave((a0, a1, a0, a3, a0, a5), low)
    for t in range(TILES):
        half = (even, odd)[t % 2][t // 2]
        amat[t * 128 : t * 128 + 128, :] = half.T.astype(bf16)
    for b in range(4):
        r = 64 + 4 * b + 3
        wide = jnp.broadcast_to(pay[OWN, r : r + 1, :], (128, 128))
        wcol[b * 128 : b * 128 + 128, :] = wide.T


def distance(t, some, at, lists, amat, bmat, dist):
    a = amat[pl.ds(pl.multiple_of(t * 128, 128), 128), :]
    tiles = [bmat[lists[0, 0, 0, t, c] + 4 * c] for c in some]
    b = tiles[0] if len(some) == 1 else jnp.concatenate(tiles, axis=1)
    dist[:, at * 128 : (at + len(some)) * 128] = dot_nn(a, b)


def one_tile(t, ahead, now, later, cells, first, lists, amat, bmat, rmat, total, gather, before=None, done=None):
    rows, groups = 32, 4
    pairs = range(0, len(cells), 2)
    for g in range(groups):
        if gather is not None:
            add_up((t + 15) & 15, [g], before, gather)
        at = pl.multiple_of(t * 128 + g * rows, rows)
        if first:
            acc = [jnp.zeros((rows, 128), f32) for _ in range(4)]
        else:
            acc = [total[k, pl.ds(at, rows), :] for k in range(4)]
        for p in pairs:
            turn = g * len(pairs) + p // 2
            if turn % groups == 0:
                q = 2 * (turn // groups)
                distance(ahead, cells[q : q + 2], q, lists, amat, bmat, later)
            for n in range(p, min(p + 2, len(cells))):
                e = 4 * (lists[0, 0, 0, t, cells[n]] + 4 * cells[n])
                s = lax.rsqrt(now[g * rows : (g + 1) * rows, n * 128 : n * 128 + 128])
                s = s * s * s
                for k in range(4):
                    line = rmat[pl.ds(e + k, 8, stride=0), :]
                    acc[k] = acc[k] + s * jnp.concatenate([line] * (rows // 8), axis=0)
        for k in range(4):
            if done is None:
                total[k, pl.ds(at, rows), :] = acc[k]
            else:
                done[k, g * rows : (g + 1) * rows, :] = acc[k]


def add_columns(gather, rows, lane0, sums):
    lane = lax.broadcasted_iota(i32, (rows.size, 128), 1)
    got = gather[rows, :]
    for k in range(4):
        got = jnp.where(lane == lane0 + k, jnp.sum(sums[k], axis=1, keepdims=True), got)
    gather[rows, :] = got


def add_up(t, groups, done, gather):
    for g in groups:
        at = pl.ds(g * 32, 32)
        add_columns(gather, at, 4 * t, [done[k, at, :] for k in range(4)])


def abs_of(x):
    return jnp.maximum(x, -x)


def when(condition, work):
    if condition is True:
        work()
    else:
        pl.when(condition)(work)


def once(p, work):
    lax.fori_loop(0, 1 + jnp.minimum(p, 0), lambda _, c: (work(), c)[1], 0)


def atomic_phase(cells, first, lists, amat, bmat, rmat, dist0, dist1, total, gather=None, done=(None, None)):
    for q in range(0, len(cells), 2):
        distance(0, cells[q : q + 2], q, lists, amat, bmat, dist0)
    shared = (cells, first, lists, amat, bmat, rmat, total, gather)

    def two_tiles(p, _):
        once(p, lambda: one_tile(2 * p, 2 * p + 1, dist0, dist1, *shared, done[1], done[0]))
        once(p, lambda: one_tile(2 * p + 1, (2 * p + 2) & 15, dist1, dist0, *shared, done[0], done[1]))
        return 0

    lax.fori_loop(0, 8, two_tiles, 0)
    if gather is not None:
        add_up(15, range(4), done[1], gather)


def bead_places(lists, b):
    return [16 * lax.shift_right_logical(lists[0, 0, 0, b, n], 2) + lists[0, 0, 0, b, n] + 16 for n in range(12)]


def bead_distances(b, n, lists, amat, bmat, dist):
    a = amat[2048 + b * 128 : 2176 + b * 128, :]
    tiles = [bmat[q] for q in bead_places(lists, b)[n : n + 2]]
    dist[:, n * 128 : n * 128 + 256] = dot_nn(a, jnp.concatenate(tiles, axis=1))


def bead_tile(b, now, later, lists, amat, bmat, rmat, wcol, gather):
    rows = 32
    places = bead_places(lists, b)
    for g in range(128 // rows):
        acc = [jnp.zeros((rows, 128), f32) for _ in range(4)]
        own = wcol[b * 128 + g * rows : b * 128 + (g + 1) * rows, :]
        for n in range(12):
            if b < 3 and n % 2 == 0 and (6 * g + n // 2) % 4 == 0:
                bead_distances(b + 1, 2 * ((6 * g + n // 2) // 4), lists, amat, bmat, later)
            line = [
                jnp.concatenate([rmat[pl.ds(4 * places[n] + k, 8, stride=0), :]] * (rows // 8), axis=0) for k in range(4)
            ]
            d = now[g * rows : (g + 1) * rows, n * 128 : n * 128 + 128]
            s = jnp.exp2((-inv_sigma_sq * log2_e) * d) * (1.0 - own * line[3])
            for k in range(3):
                acc[k] = acc[k] + s * line[k]
            acc[3] = acc[3] + s
        add_columns(gather, pl.ds(g * rows, rows), 64 + 4 * b, acc)


def coarse_phase(lists, amat, bmat, rmat, wcol, dist0, dist1, gather):
    for n in range(0, 12, 2):
        bead_distances(0, n, lists, amat, bmat, dist0)
    for b in range(4):
        bead_tile(b, (dist0, dist1)[b % 2], (dist1, dist0)[b % 2], lists, amat, bmat, rmat, wcol, gather)


def prologue(pos, charge, mass, weight, mapping, table, pay, wide16, bead16, light16, beads):
    label = mapping[0, 0, 0:1, :]

    label16 = label.astype(jnp.int16)

    def rows_of_table(k, _):
        at = pl.multiple_of(k * 32, 32)
        ids = (lax.broadcasted_iota(i32, (32, 2048), 0) + at).astype(jnp.int16)
        same = ids == jnp.broadcast_to(label16, (32, 2048))
        table[pl.ds(at, 32), :] = jnp.where(same, jnp.ones((), bf16), jnp.zeros((), bf16))
        return 0

    lax.fori_loop(0, 16, rows_of_table, 0)
    wide16[12:16, :] = jnp.zeros((4, 2048), f32)
    m = mass[0, 0, 0:1, :]
    for k in range(3):
        h, mid, l = split3(m * pos[0, 0, k, 0:1, :])
        wide16[k : k + 1, :] = h
        wide16[4 + k : 5 + k, :] = mid
        wide16[8 + k : 9 + k, :] = l
    h, mid, l = split3(m)
    wide16[3:4, :] = h
    wide16[7:8, :] = mid
    wide16[11:12, :] = l
    bead16[...] = dot_nt(wide16[...].astype(bf16), table[...])
    sums = bead16[0:4, :] + bead16[4:8, :] + bead16[8:12, :]
    beads[0:3, :] = sums[0:3] / sums[3:4]
    beads[6:7, :] = weight[0, 0, 0:1, :]
    beads[7:8, :] = sums[3:4]
    light16[...] = jnp.zeros((16, 512), f32)
    h, mid, l = split3(weight[0, 0, 0:1, :])
    light16[0:1, :] = h
    light16[1:2, :] = mid
    light16[2:3, :] = l
    atom_weight = jnp.sum(dot_nn(light16[...].astype(bf16), table[...]), axis=0, keepdims=True)
    qw = charge[0, 0, 0:1, :] * atom_weight
    for t in range(16):
        cut = slice(t * 128, t * 128 + 128)
        for k in range(3):
            pay[OWN, 4 * t + k : 4 * t + k + 1, :] = pos[0, 0, k, 0:1, cut] - 0.5
        pay[OWN, 4 * t + 3 : 4 * t + 4, :] = qw[:, cut]
    for b in range(4):
        cut = slice(b * 128, b * 128 + 128)
        pay[OWN, 64 + 4 * b : 67 + 4 * b, :] = beads[0:3, cut] - 0.5
        pay[OWN, 67 + 4 * b : 68 + 4 * b, :] = weight[0, 0, 0:1, cut]


def build_leavers(leaving, mapping, picks, leavers):
    ids = lax.broadcasted_iota(i32, (512, 128), 0)
    for way in range(2):
        row = leaving[0, 0, 0, way : way + 1, :]
        picks[:, way * 128 : way * 128 + 128] = jnp.where(ids == row, 1.0, 0.0).astype(bf16)
        column = jnp.broadcast_to(row.astype(f32), (128, 128)).T.astype(i32)
        for t in range(16):
            cut = slice(t * 128, t * 128 + 128)
            leavers[way * 128 : way * 128 + 128, cut] = jnp.where(column == mapping[0, 0, 0:1, cut], 1.0, 0.0).astype(bf16)


def epilogue(pay, gather, picks, leavers, flat, flat3, wide16, bead16, bead32, beads, parcel):
    row, _ = place()
    own = pay[OWN].reshape(10, 8, 128)
    summed = gather[...].T[0:80, :].reshape(10, 8, 128)
    force = own * fourth_to_all(summed, row) - summed
    atomic = force[:8] * fourth_to_all(own[:8], row[:8])
    flat[...] = jnp.concatenate([atomic, 2.0 * force[8:]], axis=0).reshape(80, 128)
    h, m, l = split3(atomic.reshape(64, 128))
    flat3[0] = h
    flat3[1] = m
    flat3[2] = l
    wide16[12:16, :] = jnp.zeros((4, 2048), f32)
    for t in range(16):
        cut = slice(t * 128, t * 128 + 128)
        for k in range(3):
            wide16[4 * k : 4 * k + 4, cut] = flat3[k, 4 * t : 4 * t + 4, :]
    summed = dot_nt(wide16[...].astype(bf16), leavers[...])
    for b in range(4):
        beads[3:6, b * 128 : b * 128 + 128] = flat[64 + 4 * b : 67 + 4 * b, :]
    h, m, l = split3(beads[...])
    bead32[0:8, :] = h
    bead32[8:16, :] = m
    bead32[16:24, :] = l
    bead32[24:32, :] = jnp.zeros((8, 512), f32)
    got = dot_nn(bead32[...].astype(bf16), picks[...])
    got = got[0:8] + got[8:16] + got[16:24]
    bead16[:, 0:256] = summed
    for way in range(2):
        cut = slice(way * 128, way * 128 + 128)
        parcel[way] = got[:, cut]
        parcel[way, 3:6, :] = parcel[way, 3:6, :] + (bead16[0:3, cut] + bead16[4:7, cut] + bead16[8:11, cut])
    h, m, l = split3(beads[3:6, :] / beads[7:8, :])
    bead16[...] = jnp.zeros((16, 512), f32)
    bead16[0:3, :] = h
    bead16[4:7, :] = m
    bead16[8:11, :] = l
    return bead16[...].astype(bf16)


def finish(mass, table, coarse, flat, wide16, forces):
    wide16[...] = dot_nn(coarse, table[...])
    spread = (wide16[0:3, :] + wide16[4:7, :] + wide16[8:11, :]) * mass[0, 0, 0:1, :]
    for t in range(16):
        cut = slice(t * 128, t * 128 + 128)
        got = flat[4 * t : 4 * t + 3, :] + spread[:, cut]
        for k in range(3):
            forces[0, 0, k, 0:1, cut] = got[k : k + 1]


def body(comm, *refs):
    inputs, refs = refs[:8], refs[8:]
    if not comm:
        given, refs = refs[0], refs[1:]
    (
        forces, arrivals, pos, charge, mass, weight, mapping, atom_lists, bead_lists, leaving,
        pay, bmat, rmat, amat, wcol, dist0, dist1, done0, done1, total, gather, table, wide16, bead16, light16, bead32, beads, picks, leavers, flat, flat3,
        parcel, landed, load_sem, send_sem, recv_sem, pass_send, pass_recv,
    ) = refs
    staged = (pos, charge, mass, weight, mapping, atom_lists, bead_lists, leaving)
    loads = [pltpu.make_async_copy(inputs[n], staged[n], load_sem.at[n]) for n in range(8)]
    for n in (4, 3, 2, 0, 1, 5, 6, 7):
        loads[n].start()
    if comm:
        axes = ("gx", "gy", "gz")
        me = [lax.axis_index(a) for a in axes]
        size = [lax.axis_size(a) for a in axes]

        def at(steps):
            return tuple(lax.rem(me[n] + (size[n] + steps[n]), size[n]) if steps[n] else me[n] for n in range(3))

        barrier = pltpu.get_barrier_semaphore()
        for steps in PARTNERS:
            pl.semaphore_signal(barrier, inc=1, device_id=at(steps), device_id_type=MESH)

        def send(source, target, sem, steps):
            return pltpu.make_async_remote_copy(
                src_ref=pay.at[source],
                dst_ref=pay.at[target],
                send_sem=send_sem.at[sem],
                recv_sem=recv_sem.at[sem],
                device_id=at(steps),
                device_id_type=MESH,
            )

        copies = {s: send(OWN, s, s, steps) for s, steps in ROUTE.items()}
        near = 1 - 2 * lax.rem(me[2], 2)
        other = (me[0], me[1], me[2] + near)
        far_copies, near_copies, near_arrivals = [], [], []
        for a, b in PLANE:
            side = slot_of(a, b, 0)
            far_copies.append(send(OWN - near, side - near, side - 1, (-a, -b, 0)))
            for target, group in ((side - near, near_copies), (side + near, near_arrivals)):
                group.append(
                    pltpu.make_async_remote_copy(
                        src_ref=pay.at[side],
                        dst_ref=pay.at[target],
                        send_sem=send_sem.at[side + 1],
                        recv_sem=recv_sem.at[side + 1],
                        device_id=other,
                        device_id_type=MESH,
                    )
                )
    if comm:
        away = abs_of(2 * me[0] + 1 - size[0])
        has_atomic = 10 * away < 7 * size[0]
        has_coarse = 10 * (away + 2) >= 3 * size[0]
    else:
        has_atomic = has_coarse = True
    for n in range(8):
        loads[n].wait()
    prologue(pos, charge, mass, weight, mapping, table, pay, wide16, bead16, light16, beads)
    if comm:
        pl.semaphore_wait(barrier, len(PARTNERS))
        for s in POLES + SIDES:
            copies[s].start()
    else:
        for s in POLES + SIDES + CORNERS:
            pay[s] = given[s]
    build_own(pay, amat, wcol)
    build_leavers(leaving, mapping, picks, leavers)
    build_cell(OWN, pay, bmat, rmat)
    shared = (atom_lists, amat, bmat, rmat, dist0, dist1, total)
    gather[...] = jnp.zeros((128, 128), f32)
    when(has_atomic, lambda: atomic_phase([OWN], True, *shared))
    if comm:
        for s in POLES:
            copies[s].wait_recv()
        for copy in far_copies:
            copy.start()
    for s in POLES:
        build_cell(s, pay, bmat, rmat)
    for n, s in enumerate(SIDES):
        if comm:
            copies[s].wait_recv()
            near_copies[n].start()
        build_cell(s, pay, bmat, rmat)
    when(has_atomic, lambda: atomic_phase(POLES + SIDES, False, *shared))
    if comm:
        for copy in far_copies + near_arrivals:
            copy.wait_recv()
    for s in CORNERS:
        build_cell(s, pay, bmat, rmat)
    when(has_atomic, lambda: atomic_phase(CORNERS, False, *shared, gather, (done0, done1)))
    when(has_coarse, lambda: coarse_phase(bead_lists, amat, bmat, rmat, wcol, dist0, dist1, gather))
    coarse = epilogue(pay, gather, picks, leavers, flat, flat3, wide16, bead16, bead32, beads, parcel)
    if comm:
        passes = []
        for way, step in ((0, 1), (1, -1)):
            passes.append(
                pltpu.make_async_remote_copy(
                    src_ref=parcel.at[way],
                    dst_ref=landed.at[way],
                    send_sem=pass_send.at[way],
                    recv_sem=pass_recv.at[way],
                    device_id=at((step, 0, 0)),
                    device_id_type=MESH,
                )
            )
            passes[-1].start()
        finish(mass, table, coarse, flat, wide16, forces)
        for copy in [*copies.values(), *far_copies, *near_copies]:
            copy.wait_send()
        first = lax.broadcasted_iota(i32, (8, 128), 0) == 0
        for way, move in ((0, -1.0), (1, 1.0)):
            passes[way].wait_recv()
            arrivals[0, 0, 0, way] = landed[way] + jnp.where(first, move, 0.0)
        for way in range(2):
            passes[way].wait_send()
    else:
        finish(mass, table, coarse, flat, wide16, forces)
        arrivals[0, 0, 0] = parcel[...]


def make_kernel(comm):
    vmem = pl.BlockSpec(memory_space=pltpu.VMEM)
    specs = [pl.BlockSpec(memory_space=pltpu.HBM)] * 8 + ([] if comm else [vmem])
    return pl.pallas_call(
        functools.partial(body, comm),
        out_shape=(
            jax.ShapeDtypeStruct((1, 1, 3, 1, 2048), f32),
            jax.ShapeDtypeStruct((1, 1, 1, 2, 8, 128), f32),
        ),
        in_specs=specs,
        out_specs=(vmem, vmem),
        scratch_shapes=[
            pltpu.VMEM((1, 1, 3, 1, 2048), f32),
            pltpu.VMEM((1, 1, 1, 2048), f32),
            pltpu.VMEM((1, 1, 1, 2048), f32),
            pltpu.VMEM((1, 1, 1, 512), f32),
            pltpu.VMEM((1, 1, 1, 2048), i32),
            pltpu.SMEM((1, 1, 1, 16, 27), i32),
            pltpu.SMEM((1, 1, 1, 4, 12), i32),
            pltpu.VMEM((1, 1, 1, 2, 128), i32),
            pltpu.VMEM((27, 80, 128), f32),
            pltpu.VMEM((27 * TILES, 32, 128), bf16),
            pltpu.VMEM((27 * TILES * 4, 128), f32),
            pltpu.VMEM((TILES * 128, 32), bf16),
            pltpu.VMEM((512, 128), f32),
            pltpu.VMEM((128, 16 * 128), f32),
            pltpu.VMEM((128, 16 * 128), f32),
            pltpu.VMEM((4, 128, 128), f32),
            pltpu.VMEM((4, 128, 128), f32),
            pltpu.VMEM((4, 2048, 128), f32),
            pltpu.VMEM((128, 128), f32),
            pltpu.VMEM((512, 2048), bf16),
            pltpu.VMEM((16, 2048), f32),
            pltpu.VMEM((16, 512), f32),
            pltpu.VMEM((16, 512), f32),
            pltpu.VMEM((32, 512), f32),
            pltpu.VMEM((8, 512), f32),
            pltpu.VMEM((512, 256), bf16),
            pltpu.VMEM((256, 2048), bf16),
            pltpu.VMEM((80, 128), f32),
            pltpu.VMEM((3, 64, 128), f32),
            pltpu.VMEM((2, 8, 128), f32),
            pltpu.VMEM((2, 8, 128), f32),
            pltpu.SemaphoreType.DMA((8,)),
            pltpu.SemaphoreType.DMA((27,)),
            pltpu.SemaphoreType.DMA((27,)),
            pltpu.SemaphoreType.DMA((2,)),
            pltpu.SemaphoreType.DMA((2,)),
        ],
        compiler_params=pltpu.CompilerParams(
            collective_id=0 if comm else None, has_side_effects=comm, vmem_limit_bytes=48 << 20
        ),
        name="force_step",
    )


def put_out(forces, arrivals, forces_out, arrivals_out, sem):
    copies = [
        pltpu.make_async_copy(forces, forces_out, sem.at[0]),
        pltpu.make_async_copy(arrivals, arrivals_out, sem.at[1]),
    ]
    for copy in copies:
        copy.start()
    for copy in copies:
        copy.wait()


def settle(forces, arrivals):
    vmem = pl.BlockSpec(memory_space=pltpu.VMEM)
    hbm = pl.BlockSpec(memory_space=pltpu.HBM)
    return pl.pallas_call(
        put_out,
        out_shape=(
            jax.ShapeDtypeStruct(forces.shape, f32),
            jax.ShapeDtypeStruct(arrivals.shape, f32),
        ),
        in_specs=[vmem, vmem],
        out_specs=(hbm, hbm),
        scratch_shapes=[pltpu.SemaphoreType.DMA((2,))],
        compiler_params=pltpu.CompilerParams(vmem_limit_bytes=8 << 20),
        name="settle",
    )(forces, arrivals)


def solution(mesh):
    def cell(*dims):
        return P("gx", "gy", "gz", *[None] * len(dims))

    placed = (cell(0, 0), cell(0), cell(0), cell(0), cell(0), cell(0, 0), cell(0, 0), cell(0, 0))
    def step(positions, *rest):
        operands = [pltpu.with_memory_space_constraint(x, pltpu.HBM) for x in (jnp.swapaxes(positions, 2, 3), *rest)]
        forces, arrivals = settle(*make_kernel(True)(*operands))
        return jnp.swapaxes(forces, 2, 3), arrivals

    return jax.shard_map(
        step,
        mesh=mesh,
        in_specs=placed,
        out_specs=(cell(0, 0), cell(0, 0, 0)),
        check_vma=False,
    )
```

```python
import functools

import jax
import jax.numpy as jnp
from jax import lax
from jax.experimental import pallas as pl
from jax.experimental.pallas import tpu as pltpu
from jax.sharding import PartitionSpec as P

soft_core = 0.01
inv_sigma_sq = 4.0
log2_e = 1.4426950408889634
f32, bf16, i32 = jnp.float32, jnp.bfloat16, jnp.int32
MESH = pl.DeviceIdType.MESH
TILES = 20


def slot_of(a, b, c):
    return 9 * (a + 1) + 3 * (b + 1) + (c + 1)


OWN = slot_of(0, 0, 0)
PLANE = [(a, b) for a in (-1, 0, 1) for b in (-1, 0, 1) if a or b]
POLES = [slot_of(0, 0, c) for c in (-1, 1)]
SIDES = [slot_of(a, b, 0) for a, b in PLANE]
CORNERS = [slot_of(a, b, c) for a, b in PLANE for c in (-1, 1)]
ROUTE = {slot_of(0, 0, c): (0, 0, -c) for c in (-1, 1)}
ROUTE |= {slot_of(a, b, 0): (-a, -b, 0) for a, b in PLANE}
PARTNERS = [(0, 0, -1), (0, 0, 1)] + [(a, b, 0) for a, b in PLANE]


def split3(v):
    h = v.astype(bf16).astype(f32)
    r = v - h
    m = r.astype(bf16).astype(f32)
    return h, m, r - m


def dot_nt(a, b):
    return lax.dot_general(a, b, (((1,), (1,)), ((), ())), preferred_element_type=f32)


def dot_nn(a, b):
    return jnp.dot(a, b, preferred_element_type=f32)


def stack3(scr, rows, value):
    h, m, l = split3(value)
    scr[0:rows, :] = h
    scr[rows : 2 * rows, :] = m
    scr[2 * rows : 3 * rows, :] = l


def place():
    sub = lax.broadcasted_iota(i32, (10, 8, 128), 1)
    return sub & 3, sub < 4


def up_rows(x, by):
    return pltpu.roll(x, by % 8, 1)


def fourth_to_all(v, row):
    u = jnp.where(row == 3, v, 0.0)
    u = u + up_rows(u, -1)
    return u + up_rows(u, -2)


def squares_to_fourth(v):
    sq = v * v
    return up_rows(sq, 1) + up_rows(sq, 2) + up_rows(sq, 3)


def interleave(groups, low):
    even, odd = [], []
    for g, k in zip(groups[0::2], groups[1::2], strict=True):
        even.append(jnp.where(low, g, up_rows(k, 4)))
        odd.append(jnp.where(low, up_rows(g, 4), k))
    zero = jnp.zeros((10, 8, 128), f32)
    return (
        jnp.concatenate(even + [zero], axis=1),
        jnp.concatenate(odd + [zero], axis=1),
    )


def build_cell(slot, pay, bmat, rmat):
    row, low = place()
    v = pay[slot].reshape(10, 8, 128)
    offset = (slot // 9 - 1, slot // 3 % 3 - 1, slot % 3 - 1)
    for axis in range(3):
        if offset[axis]:
            v = v + jnp.where(row == axis, float(offset[axis]), 0.0)
    atoms, beads = v[:8], v[8:]
    scaled = jnp.where(row[:8] == 3, atoms, atoms * fourth_to_all(atoms, row[:8]))
    rmat[pl.ds(slot * TILES * 4, 64), :] = scaled.reshape(64, 128)
    rmat[pl.ds(slot * TILES * 4 + 64, 16), :] = beads.reshape(16, 128)
    h, m, l = split3(jnp.where(row == 3, squares_to_fourth(v), v))
    h1 = jnp.where(row == 3, 1.0, h)
    m1 = jnp.where(row == 3, 1.0, m)
    even, odd = interleave((h, h1, m, m1, l, h1), low)
    even, odd = even.astype(bf16), odd.astype(bf16)
    for k in range(10):
        bmat[slot * TILES + 2 * k] = even[k]
        bmat[slot * TILES + 2 * k + 1] = odd[k]


def build_own(pay, amat, wcol):
    row, low = place()
    v = pay[OWN].reshape(10, 8, 128)
    atom = lax.broadcasted_iota(i32, (10, 8, 128), 0) < 8
    near = squares_to_fourth(v) + jnp.where(atom, soft_core, 0.0)
    h, m, l = split3(jnp.where(row == 3, near, v))
    a0 = jnp.where(row == 3, 1.0, -2.0 * h)
    a1 = jnp.where(row == 3, h, -2.0 * m)
    a3 = jnp.where(row == 3, m, -2.0 * m)
    a5 = jnp.where(row == 3, l, -2.0 * l)
    even, odd = interleave((a0, a1, a0, a3, a0, a5), low)
    for t in range(TILES):
        half = (even, odd)[t % 2][t // 2]
        amat[t * 128 : t * 128 + 128, :] = half.T.astype(bf16)
    for b in range(4):
        r = 64 + 4 * b + 3
        wide = jnp.broadcast_to(pay[OWN, r : r + 1, :], (128, 128))
        wcol[b * 128 : b * 128 + 128, :] = wide.T


def distance(t, some, at, lists, amat, bmat, dist):
    a = amat[pl.ds(pl.multiple_of(t * 128, 128), 128), :]
    tiles = [bmat[lists[0, 0, 0, t, c] + 4 * c] for c in some]
    b = tiles[0] if len(some) == 1 else jnp.concatenate(tiles, axis=1)
    dist[:, at * 128 : (at + len(some)) * 128] = dot_nn(a, b)


def one_tile(t, ahead, now, later, cells, first, lists, amat, bmat, rmat, total, gather, before=None, done=None):
    rows, groups = 32, 4
    pairs = range(0, len(cells), 2)
    for g in range(groups):
        if gather is not None:
            add_up((t + 15) & 15, [g], before, gather)
        at = pl.multiple_of(t * 128 + g * rows, rows)
        if first:
            acc = [jnp.zeros((rows, 128), f32) for _ in range(4)]
        else:
            acc = [total[k, pl.ds(at, rows), :] for k in range(4)]
        for p in pairs:
            turn = g * len(pairs) + p // 2
            if turn % groups == 0:
                q = 2 * (turn // groups)
                distance(ahead, cells[q : q + 2], q, lists, amat, bmat, later)
            for n in range(p, min(p + 2, len(cells))):
                e = 4 * (lists[0, 0, 0, t, cells[n]] + 4 * cells[n])
                s = lax.rsqrt(now[g * rows : (g + 1) * rows, n * 128 : n * 128 + 128])
                s = s * s * s
                for k in range(4):
                    line = rmat[pl.ds(e + k, 8, stride=0), :]
                    acc[k] = acc[k] + s * jnp.concatenate([line] * (rows // 8), axis=0)
        for k in range(4):
            if done is None:
                total[k, pl.ds(at, rows), :] = acc[k]
            else:
                done[k, g * rows : (g + 1) * rows, :] = acc[k]


def add_columns(gather, rows, lane0, sums):
    lane = lax.broadcasted_iota(i32, (rows.size, 128), 1)
    got = gather[rows, :]
    for k in range(4):
        got = jnp.where(lane == lane0 + k, jnp.sum(sums[k], axis=1, keepdims=True), got)
    gather[rows, :] = got


def add_up(t, groups, done, gather):
    for g in groups:
        at = pl.ds(g * 32, 32)
        add_columns(gather, at, 4 * t, [done[k, at, :] for k in range(4)])


def abs_of(x):
    return jnp.maximum(x, -x)


def when(condition, work):
    if condition is True:
        work()
    else:
        pl.when(condition)(work)


def once(p, work):
    lax.fori_loop(0, 1 + jnp.minimum(p, 0), lambda _, c: (work(), c)[1], 0)


def atomic_phase(cells, first, lists, amat, bmat, rmat, dist0, dist1, total, gather=None, done=(None, None)):
    for q in range(0, len(cells), 2):
        distance(0, cells[q : q + 2], q, lists, amat, bmat, dist0)
    shared = (cells, first, lists, amat, bmat, rmat, total, gather)

    def two_tiles(p, _):
        once(p, lambda: one_tile(2 * p, 2 * p + 1, dist0, dist1, *shared, done[1], done[0]))
        once(p, lambda: one_tile(2 * p + 1, (2 * p + 2) & 15, dist1, dist0, *shared, done[0], done[1]))
        return 0

    lax.fori_loop(0, 8, two_tiles, 0)
    if gather is not None:
        add_up(15, range(4), done[1], gather)


def bead_places(lists, b):
    return [16 * lax.shift_right_logical(lists[0, 0, 0, b, n], 2) + lists[0, 0, 0, b, n] + 16 for n in range(12)]


def bead_distances(b, n, lists, amat, bmat, dist):
    a = amat[2048 + b * 128 : 2176 + b * 128, :]
    tiles = [bmat[q] for q in bead_places(lists, b)[n : n + 2]]
    dist[:, n * 128 : n * 128 + 256] = dot_nn(a, jnp.concatenate(tiles, axis=1))


def bead_tile(b, now, later, lists, amat, bmat, rmat, wcol, gather):
    rows = 32
    places = bead_places(lists, b)
    for g in range(128 // rows):
        acc = [jnp.zeros((rows, 128), f32) for _ in range(4)]
        own = wcol[b * 128 + g * rows : b * 128 + (g + 1) * rows, :]
        for n in range(12):
            if b < 3 and n % 2 == 0 and (6 * g + n // 2) % 4 == 0:
                bead_distances(b + 1, 2 * ((6 * g + n // 2) // 4), lists, amat, bmat, later)
            line = [
                jnp.concatenate([rmat[pl.ds(4 * places[n] + k, 8, stride=0), :]] * (rows // 8), axis=0) for k in range(4)
            ]
            d = now[g * rows : (g + 1) * rows, n * 128 : n * 128 + 128]
            s = jnp.exp2((-inv_sigma_sq * log2_e) * d) * (1.0 - own * line[3])
            for k in range(3):
                acc[k] = acc[k] + s * line[k]
            acc[3] = acc[3] + s
        add_columns(gather, pl.ds(g * rows, rows), 64 + 4 * b, acc)


def coarse_phase(lists, amat, bmat, rmat, wcol, dist0, dist1, gather):
    for n in range(0, 12, 2):
        bead_distances(0, n, lists, amat, bmat, dist0)
    for b in range(4):
        bead_tile(b, (dist0, dist1)[b % 2], (dist1, dist0)[b % 2], lists, amat, bmat, rmat, wcol, gather)


def prologue(pos, charge, mass, weight, mapping, table, pay, wide16, bead16, folded, beads):
    label = mapping[0, 0, 0:1, :]
    label16 = label.astype(jnp.int16)

    def rows_of_table(k, _):
        at = pl.multiple_of(k * 32, 32)
        ids = (lax.broadcasted_iota(i32, (32, 2048), 0) + at).astype(jnp.int16)
        same = ids == jnp.broadcast_to(label16, (32, 2048))
        table[pl.ds(at, 32), :] = jnp.where(same, jnp.ones((), bf16), jnp.zeros((), bf16))
        return 0

    lax.fori_loop(0, 16, rows_of_table, 0)
    for g in range(16):
        h, mid, l = split3(weight[0, 0, 0:1, g * 32 : g * 32 + 32])
        folded[g : g + 1, 0:32] = h
        folded[16 + g : 17 + g, 0:32] = mid
        folded[32 + g : 33 + g, 0:32] = l
    member = lax.broadcasted_iota(i32, (32, 2048), 0) == (label & 31)
    got = dot_nn(folded[:, 0:32].astype(bf16), jnp.where(member, 1.0, 0.0).astype(bf16))
    got = got[0:16] + got[16:32] + got[32:48]
    group = lax.broadcasted_iota(i32, (16, 2048), 0) == lax.shift_right_logical(label, 5)
    atom_weight = jnp.sum(jnp.where(group, got, 0.0), axis=0, keepdims=True)
    qw = charge[0, 0, 0:1, :] * atom_weight
    for t in range(16):
        cut = slice(t * 128, t * 128 + 128)
        for k in range(3):
            pay[OWN, 4 * t + k : 4 * t + k + 1, :] = pos[0, 0, k, 0:1, cut] - 0.5
        pay[OWN, 4 * t + 3 : 4 * t + 4, :] = qw[:, cut]

    wide16[12:16, :] = jnp.zeros((4, 2048), f32)
    m = mass[0, 0, 0:1, :]
    for k in range(3):
        h, mid, l = split3(m * pos[0, 0, k, 0:1, :])
        wide16[k : k + 1, :] = h
        wide16[4 + k : 5 + k, :] = mid
        wide16[8 + k : 9 + k, :] = l
    h, mid, l = split3(m)
    wide16[3:4, :] = h
    wide16[7:8, :] = mid
    wide16[11:12, :] = l
    bead16[...] = dot_nt(wide16[...].astype(bf16), table[...])
    sums = bead16[0:4, :] + bead16[4:8, :] + bead16[8:12, :]
    beads[0:3, :] = sums[0:3] / sums[3:4]
    beads[6:7, :] = weight[0, 0, 0:1, :]
    beads[7:8, :] = sums[3:4]
    for b in range(4):
        cut = slice(b * 128, b * 128 + 128)
        pay[OWN, 64 + 4 * b : 67 + 4 * b, :] = beads[0:3, cut] - 0.5
        pay[OWN, 67 + 4 * b : 68 + 4 * b, :] = weight[0, 0, 0:1, cut]


def build_leavers(leaving, mapping, picks, leavers):
    ids = lax.broadcasted_iota(i32, (512, 128), 0)
    for way in range(2):
        row = leaving[0, 0, 0, way : way + 1, :]
        picks[:, way * 128 : way * 128 + 128] = jnp.where(ids == row, 1.0, 0.0).astype(bf16)
        column = jnp.broadcast_to(row.astype(f32), (128, 128)).T.astype(i32)
        for t in range(16):
            cut = slice(t * 128, t * 128 + 128)
            leavers[way * 128 : way * 128 + 128, cut] = jnp.where(column == mapping[0, 0, 0:1, cut], 1.0, 0.0).astype(bf16)


def epilogue(pay, gather, picks, leavers, flat, flat3, wide16, bead16, bead32, beads, parcel):
    row, _ = place()
    own = pay[OWN].reshape(10, 8, 128)
    summed = gather[...].T[0:80, :].reshape(10, 8, 128)
    force = own * fourth_to_all(summed, row) - summed
    atomic = force[:8] * fourth_to_all(own[:8], row[:8])
    flat[...] = jnp.concatenate([atomic, 2.0 * force[8:]], axis=0).reshape(80, 128)
    h, m, l = split3(atomic.reshape(64, 128))
    flat3[0] = h
    flat3[1] = m
    flat3[2] = l
    wide16[12:16, :] = jnp.zeros((4, 2048), f32)
    for t in range(16):
        cut = slice(t * 128, t * 128 + 128)
        for k in range(3):
            wide16[4 * k : 4 * k + 4, cut] = flat3[k, 4 * t : 4 * t + 4, :]
    summed = dot_nt(wide16[...].astype(bf16), leavers[...])
    for b in range(4):
        beads[3:6, b * 128 : b * 128 + 128] = flat[64 + 4 * b : 67 + 4 * b, :]
    h, m, l = split3(beads[...])
    bead32[0:8, :] = h
    bead32[8:16, :] = m
    bead32[16:24, :] = l
    bead32[24:32, :] = jnp.zeros((8, 512), f32)
    got = dot_nn(bead32[...].astype(bf16), picks[...])
    got = got[0:8] + got[8:16] + got[16:24]
    bead16[:, 0:256] = summed
    for way in range(2):
        cut = slice(way * 128, way * 128 + 128)
        parcel[way] = got[:, cut]
        parcel[way, 3:6, :] = parcel[way, 3:6, :] + (bead16[0:3, cut] + bead16[4:7, cut] + bead16[8:11, cut])
    h, m, l = split3(beads[3:6, :] / beads[7:8, :])
    bead16[...] = jnp.zeros((16, 512), f32)
    bead16[0:3, :] = h
    bead16[4:7, :] = m
    bead16[8:11, :] = l
    return bead16[...].astype(bf16)


def finish(mass, table, coarse, flat, wide16, forces):
    wide16[...] = dot_nn(coarse, table[...])
    spread = (wide16[0:3, :] + wide16[4:7, :] + wide16[8:11, :]) * mass[0, 0, 0:1, :]
    for t in range(16):
        cut = slice(t * 128, t * 128 + 128)
        got = flat[4 * t : 4 * t + 3, :] + spread[:, cut]
        for k in range(3):
            forces[0, 0, k, 0:1, cut] = got[k : k + 1]


def body(comm, *refs):
    inputs, refs = refs[:8], refs[8:]
    if not comm:
        given, refs = refs[0], refs[1:]
    (
        forces, arrivals, pos, charge, mass, weight, mapping, atom_lists, bead_lists, leaving,
        pay, bmat, rmat, amat, wcol, dist0, dist1, done0, done1, total, gather, table, wide16, bead16, folded, bead32, beads, picks, leavers, flat, flat3,
        parcel, landed, load_sem, send_sem, recv_sem, pass_send, pass_recv,
    ) = refs
    staged = (pos, charge, mass, weight, mapping, atom_lists, bead_lists, leaving)
    loads = [pltpu.make_async_copy(inputs[n], staged[n], load_sem.at[n]) for n in range(8)]
    for n in (4, 3, 2, 0, 1, 5, 6, 7):
        loads[n].start()
    if comm:
        axes = ("gx", "gy", "gz")
        me = [lax.axis_index(a) for a in axes]
        size = [lax.axis_size(a) for a in axes]

        def at(steps):
            return tuple(lax.rem(me[n] + (size[n] + steps[n]), size[n]) if steps[n] else me[n] for n in range(3))

        barrier = pltpu.get_barrier_semaphore()
        for steps in PARTNERS:
            pl.semaphore_signal(barrier, inc=1, device_id=at(steps), device_id_type=MESH)

        def send(source, target, sem, steps):
            return pltpu.make_async_remote_copy(
                src_ref=pay.at[source],
                dst_ref=pay.at[target],
                send_sem=send_sem.at[sem],
                recv_sem=recv_sem.at[sem],
                device_id=at(steps),
                device_id_type=MESH,
            )

        copies = {s: send(OWN, s, s, steps) for s, steps in ROUTE.items()}
        near = 1 - 2 * lax.rem(me[2], 2)
        other = (me[0], me[1], me[2] + near)
        far_copies, near_copies, near_arrivals = [], [], []
        for a, b in PLANE:
            side = slot_of(a, b, 0)
            far_copies.append(send(OWN - near, side - near, side - 1, (-a, -b, 0)))
            for target, group in ((side - near, near_copies), (side + near, near_arrivals)):
                group.append(
                    pltpu.make_async_remote_copy(
                        src_ref=pay.at[side],
                        dst_ref=pay.at[target],
                        send_sem=send_sem.at[side + 1],
                        recv_sem=recv_sem.at[side + 1],
                        device_id=other,
                        device_id_type=MESH,
                    )
                )
    if comm:
        away = abs_of(2 * me[0] + 1 - size[0])
        has_atomic = 10 * away < 7 * size[0]
        has_coarse = 10 * (away + 2) >= 3 * size[0]
    else:
        has_atomic = has_coarse = True
    for n in range(8):
        loads[n].wait()
    prologue(pos, charge, mass, weight, mapping, table, pay, wide16, bead16, folded, beads)
    if comm:
        pl.semaphore_wait(barrier, len(PARTNERS))
        for s in POLES + SIDES:
            copies[s].start()
    else:
        for s in POLES + SIDES + CORNERS:
            pay[s] = given[s]
    build_own(pay, amat, wcol)
    build_leavers(leaving, mapping, picks, leavers)
    build_cell(OWN, pay, bmat, rmat)
    shared = (atom_lists, amat, bmat, rmat, dist0, dist1, total)
    gather[...] = jnp.zeros((128, 128), f32)
    when(has_atomic, lambda: atomic_phase([OWN], True, *shared))
    if comm:
        for s in POLES:
            copies[s].wait_recv()
        for copy in far_copies:
            copy.start()
    for s in POLES:
        build_cell(s, pay, bmat, rmat)
    for n, s in enumerate(SIDES):
        if comm:
            copies[s].wait_recv()
            near_copies[n].start()
        build_cell(s, pay, bmat, rmat)
    when(has_atomic, lambda: atomic_phase(POLES + SIDES, False, *shared))
    if comm:
        for copy in far_copies + near_arrivals:
            copy.wait_recv()
    for s in CORNERS:
        build_cell(s, pay, bmat, rmat)
    when(has_atomic, lambda: atomic_phase(CORNERS, False, *shared, gather, (done0, done1)))
    when(has_coarse, lambda: coarse_phase(bead_lists, amat, bmat, rmat, wcol, dist0, dist1, gather))
    coarse = epilogue(pay, gather, picks, leavers, flat, flat3, wide16, bead16, bead32, beads, parcel)
    if comm:
        passes = []
        for way, step in ((0, 1), (1, -1)):
            passes.append(
                pltpu.make_async_remote_copy(
                    src_ref=parcel.at[way],
                    dst_ref=landed.at[way],
                    send_sem=pass_send.at[way],
                    recv_sem=pass_recv.at[way],
                    device_id=at((step, 0, 0)),
                    device_id_type=MESH,
                )
            )
            passes[-1].start()
        finish(mass, table, coarse, flat, wide16, forces)
        for copy in [*copies.values(), *far_copies, *near_copies]:
            copy.wait_send()
        first = lax.broadcasted_iota(i32, (8, 128), 0) == 0
        for way, move in ((0, -1.0), (1, 1.0)):
            passes[way].wait_recv()
            arrivals[0, 0, 0, way] = landed[way] + jnp.where(first, move, 0.0)
        for way in range(2):
            passes[way].wait_send()
    else:
        finish(mass, table, coarse, flat, wide16, forces)
        arrivals[0, 0, 0] = parcel[...]


def make_kernel(comm):
    vmem = pl.BlockSpec(memory_space=pltpu.VMEM)
    specs = [pl.BlockSpec(memory_space=pltpu.HBM)] * 8 + ([] if comm else [vmem])
    return pl.pallas_call(
        functools.partial(body, comm),
        out_shape=(
            jax.ShapeDtypeStruct((1, 1, 3, 1, 2048), f32),
            jax.ShapeDtypeStruct((1, 1, 1, 2, 8, 128), f32),
        ),
        in_specs=specs,
        out_specs=(vmem, vmem),
        scratch_shapes=[
            pltpu.VMEM((1, 1, 3, 1, 2048), f32),
            pltpu.VMEM((1, 1, 1, 2048), f32),
            pltpu.VMEM((1, 1, 1, 2048), f32),
            pltpu.VMEM((1, 1, 1, 512), f32),
            pltpu.VMEM((1, 1, 1, 2048), i32),
            pltpu.SMEM((1, 1, 1, 16, 27), i32),
            pltpu.SMEM((1, 1, 1, 4, 12), i32),
            pltpu.VMEM((1, 1, 1, 2, 128), i32),
            pltpu.VMEM((27, 80, 128), f32),
            pltpu.VMEM((27 * TILES, 32, 128), bf16),
            pltpu.VMEM((27 * TILES * 4, 128), f32),
            pltpu.VMEM((TILES * 128, 32), bf16),
            pltpu.VMEM((512, 128), f32),
            pltpu.VMEM((128, 16 * 128), f32),
            pltpu.VMEM((128, 16 * 128), f32),
            pltpu.VMEM((4, 128, 128), f32),
            pltpu.VMEM((4, 128, 128), f32),
            pltpu.VMEM((4, 2048, 128), f32),
            pltpu.VMEM((128, 128), f32),
            pltpu.VMEM((512, 2048), bf16),
            pltpu.VMEM((16, 2048), f32),
            pltpu.VMEM((16, 512), f32),
            pltpu.VMEM((48, 128), f32),
            pltpu.VMEM((32, 512), f32),
            pltpu.VMEM((8, 512), f32),
            pltpu.VMEM((512, 256), bf16),
            pltpu.VMEM((256, 2048), bf16),
            pltpu.VMEM((80, 128), f32),
            pltpu.VMEM((3, 64, 128), f32),
            pltpu.VMEM((2, 8, 128), f32),
            pltpu.VMEM((2, 8, 128), f32),
            pltpu.SemaphoreType.DMA((8,)),
            pltpu.SemaphoreType.DMA((27,)),
            pltpu.SemaphoreType.DMA((27,)),
            pltpu.SemaphoreType.DMA((2,)),
            pltpu.SemaphoreType.DMA((2,)),
        ],
        compiler_params=pltpu.CompilerParams(
            collective_id=0 if comm else None, has_side_effects=comm, vmem_limit_bytes=48 << 20
        ),
        name="force_step",
    )


def put_out(forces, arrivals, forces_out, arrivals_out, sem):
    copies = [
        pltpu.make_async_copy(forces, forces_out, sem.at[0]),
        pltpu.make_async_copy(arrivals, arrivals_out, sem.at[1]),
    ]
    for copy in copies:
        copy.start()
    for copy in copies:
        copy.wait()


def settle(forces, arrivals):
    vmem = pl.BlockSpec(memory_space=pltpu.VMEM)
    hbm = pl.BlockSpec(memory_space=pltpu.HBM)
    return pl.pallas_call(
        put_out,
        out_shape=(
            jax.ShapeDtypeStruct(forces.shape, f32),
            jax.ShapeDtypeStruct(arrivals.shape, f32),
        ),
        in_specs=[vmem, vmem],
        out_specs=(hbm, hbm),
        scratch_shapes=[pltpu.SemaphoreType.DMA((2,))],
        compiler_params=pltpu.CompilerParams(vmem_limit_bytes=8 << 20),
        name="settle",
    )(forces, arrivals)


def solution(mesh):
    def cell(*dims):
        return P("gx", "gy", "gz", *[None] * len(dims))

    placed = (cell(0, 0), cell(0), cell(0), cell(0), cell(0), cell(0, 0), cell(0, 0), cell(0, 0))
    def step(positions, *rest):
        operands = [pltpu.with_memory_space_constraint(x, pltpu.HBM) for x in (jnp.swapaxes(positions, 2, 3), *rest)]
        forces, arrivals = settle(*make_kernel(True)(*operands))
        return jnp.swapaxes(forces, 2, 3), arrivals

    return jax.shard_map(
        step,
        mesh=mesh,
        in_specs=placed,
        out_specs=(cell(0, 0), cell(0, 0, 0)),
        check_vma=False,
    )
```
